512 devices in a mesh: ch: 64 (over z_hi, y, x), ta: 8 (over z_lo, core).
Axes of the slice: x: 4, y: 8, z: 8 (z_hi: 2, z_lo: 4; z = z_hi * 4 + z_lo), core: 2. Of those that a mesh axis runs over, the one named last changes fastest.
Arguments:
- raw_strain: float32 [8192, 12288], P('ch', 'ta'), may hold values from -6 to 6
- band_index: int32 [8192], P('ch'), may hold values from 0 to 3
- filter_taps: float32 [4, 33], replicated, may hold values from -1 to 1
Outputs:
- correlation: float32 [2, 65, 8192, 128], P(None, None, ('ch', 'ta'))
The draws below stay inside these ranges and needn't reach their ends.
All inputs are finite; a program needn't handle non-finite values.
Results may differ from the reference program's by a relative error of at most 0.0037.
Values may be sent and summed in bfloat16 or wider, within the bound.
No kernel may reach another device: no remote copies, remote signals or barrier semaphores. Data moves between devices by JAX's collectives and lax.ppermute only.
A program may use at most 64 MiB of HBM per device.

```python
import math
import jax
import jax.numpy as jnp
from jax import lax

CH_DEV = 128
HF = 16
TAPS = 33
NBANDS = 4
LAGH = 32
LAGS = 65
ROUNDS = 2
RH = 1536
CHANNELS = 8192
SAMPLES = 12288
N_CH = 64


def with_ends(entries, key, least, largest):
    place = [jax.random.randint(jax.random.fold_in(key, axis), (), 0, length) for axis, length in enumerate(entries.shape)]
    main_axis = entries.shape.index(max(entries.shape))
    next_to = place[:main_axis] + [(place[main_axis] + 1) % entries.shape[main_axis]] + place[main_axis + 1:]
    return entries.at[tuple(place)].set(least).at[tuple(next_to)].set(largest)


def steps_of(key, shape, pieces, low, high):
    def one(axis_at, parts):
        heights = jax.random.uniform(jax.random.fold_in(jax.random.fold_in(key, 6), axis_at), (parts,), jnp.float32, low / len(pieces), high / len(pieces))
        return jnp.repeat(jnp.exp(heights), shape[axis_at] // parts).reshape((-1,) + (1,) * (len(shape) - axis_at - 1))

    loudness = one(*pieces[0])
    for cut in pieces[1:]:
        loudness = loudness * one(*cut)
    return loudness


def scatter_about(own_key, shape, deviation, reach, shards=(), kind=jnp.bfloat16):
    array = deviation * jax.random.normal(own_key, shape, jnp.float32)
    if shards:
        array = array * steps_of(own_key, shape, shards, -0.22, 0.18)
    return jnp.clip(array, -reach, reach).astype(kind)


def setup_inputs(seed: int = 0) -> dict:
    key_list = jax.random.split(jax.random.key(seed), 4)
    return {
        "raw_strain": scatter_about(key_list[0], (CHANNELS, SAMPLES), 1.0, 6.0, ((0, 64), (1, 8)), jnp.float32),
        "band_index": with_ends(jax.random.randint(key_list[1], (CHANNELS,), 0, NBANDS), jax.random.fold_in(key_list[1], 1), 0, NBANDS - 1).astype(jnp.int32),
        "filter_taps": scatter_about(key_list[2], (NBANDS, TAPS), TAPS ** -0.5, 1.0, (), jnp.float32),
    }


def reference(raw_strain, band_index, filter_taps):
    coeffs = filter_taps[band_index]
    padded = jnp.pad(raw_strain, ((0, 0), (HF, HF)))
    filtered = jnp.zeros_like(raw_strain)
    for step in range(TAPS):
        filtered = filtered + coeffs[:, step:step + 1] * padded[:, step:step + SAMPLES]
    magnitude = jnp.abs(filtered)
    cumulative = jnp.concatenate([jnp.zeros((CHANNELS, 1), jnp.float32), jnp.cumsum(magnitude, axis=1)], axis=1)
    times = jnp.arange(SAMPLES, dtype=jnp.int32)
    upper = jnp.minimum(times + RH, SAMPLES - 1) + 1
    lower = jnp.maximum(times - RH, 0)
    window_sum = jnp.take(cumulative, upper, axis=1) - jnp.take(cumulative, lower, axis=1)
    counted = (upper - lower).astype(jnp.float32)
    level = window_sum / counted[None, :]
    normalized = (filtered / (level + 1e-06)).astype(jnp.bfloat16)
    values = normalized.astype(jnp.float32)
    blocks = values.reshape(N_CH, CH_DEV, SAMPLES)
    shifted_pad = jnp.pad(blocks, ((0, 0), (0, 0), (LAGH, LAGH)))
    scale = 1.0 / math.sqrt(SAMPLES)
    rounds_out = []
    for round_id in range(ROUNDS):
        offset = (round_id + 1) * (N_CH // 4)
        partner = jnp.roll(blocks, offset, axis=0)

        def one_lag(lag):
            start = (2 * LAGH - lag).astype(jnp.int32)
            moved = lax.dynamic_slice_in_dim(shifted_pad, start, SAMPLES, 2)
            return jnp.einsum('bit,bjt->bij', moved, partner).reshape(CHANNELS, CH_DEV) * scale
        rounds_out.append(lax.map(one_lag, jnp.arange(LAGS, dtype=jnp.int32)))
    return jnp.stack(rounds_out)
```

```python
import functools
import math

import jax
import jax.numpy as jnp
from jax import lax
from jax.experimental import pallas as pl
from jax.experimental.pallas import tpu as pltpu
from jax.sharding import PartitionSpec as P

HF = 16
TAPS = 33
NBANDS = 4
LAGH = 32
LAGS = 65
ROUNDS = 2
EDGE = 128
GROUP = 13
AXES = ("ch", "ta")


class Layout:
    def __init__(self):
        self.blocks = lax.axis_size("ch")
        self.slices = lax.axis_size("ta")
        self.cols = self.blocks // 2
        self.depth = self.slices // 2
        self.ring = 2 * self.depth

    def index(self, pos, col, core):
        zh, zl = divmod(pos % self.ring, self.depth)
        return (zh * self.cols + col) * self.slices + zl * 2 + core

    def every(self):
        for pos in range(self.ring):
            for col in range(self.cols):
                for core in range(2):
                    yield pos, col, core

    def from_ring(self, step):
        return [(self.index(p + step, c, k), self.index(p, c, k)) for p, c, k in self.every()]

    def swap_columns(self):
        return [
            (self.index(p, (c + self.cols // 2) % self.cols, k), self.index(p, c, k))
            for p, c, k in self.every()
        ]

    def swap_cores(self):
        return [(self.index(p, c, 1 - k), self.index(p, c, k)) for p, c, k in self.every()]


def to_neighbours(low_part, high_part):
    count = lax.axis_size("ta")
    forward = [(i, i + 1) for i in range(count - 1)]
    backward = [(i + 1, i) for i in range(count - 1)]
    from_low = lax.ppermute(high_part, "ta", forward)
    from_high = lax.ppermute(low_part, "ta", backward)
    return from_low, from_high


def normalize(raw, band_index, filter_taps):
    length = raw.shape[1]
    time_groups = lax.axis_size("ta")
    whole_len = length * time_groups
    onehot = (band_index[:, None] == jnp.arange(NBANDS, dtype=jnp.int32)[None, :]).astype(
        jnp.float32
    )
    coeffs = jnp.dot(
        onehot, filter_taps, precision=lax.Precision.HIGHEST, preferred_element_type=jnp.float32
    )
    low, high = to_neighbours(raw[:, :HF], raw[:, length - HF :])
    extended = jnp.concatenate([low, raw, high], axis=1)
    filtered = jnp.zeros_like(raw)
    for step in range(TAPS):
        filtered = filtered + coeffs[:, step : step + 1] * extended[:, step : step + length]
    magnitude = jnp.abs(filtered)
    prefix = jnp.cumsum(magnitude, axis=1)
    total = prefix[:, length - 1 :]
    suffix = total - prefix + magnitude
    before, after = to_neighbours(prefix, suffix)
    window_sum = before + total + after
    global_time = lax.axis_index("ta") * length + jnp.arange(length, dtype=jnp.int32)
    upper = jnp.minimum(global_time + length, whole_len - 1) + 1
    lower = jnp.maximum(global_time - length, 0)
    counted = (upper - lower).astype(jnp.float32)
    level = window_sum / counted[None, :]
    return (filtered / (level + 1e-06)).astype(jnp.bfloat16)


def gather_ring(layout, piece):
    ring = layout.ring
    slots = {0: (piece,)}
    up = down = piece
    for step in range(1, ring // 2):
        up = lax.ppermute(up, AXES, layout.from_ring(1))
        down = lax.ppermute(down, AXES, layout.from_ring(-1))
        slots[step] = (up,)
        slots[ring - step] = (down,)
    half = piece.shape[0] // 2
    slots[ring // 2] = (
        lax.ppermute(up[:half], AXES, layout.from_ring(1)),
        lax.ppermute(down[half:], AXES, layout.from_ring(-1)),
    )
    return slots


def lagged_kernel(layout, rows, length, scale, *refs):
    place_ref, edge_ref = refs[:2]
    ring, depth = layout.ring, layout.depth
    flat = list(refs[2 : 2 + 2 * (ring + 1)])
    own_slots, swap_slots = {}, {}
    for slots in (own_slots, swap_slots):
        for d in range(ring):
            count = 2 if d == ring // 2 else 1
            slots[d] = [flat.pop(0) for _ in range(count)]
    mine_ref, other_ref, own_buf, part_buf, acc, own_sem, near_sem, far_sem = refs[
        2 + 2 * (ring + 1) :
    ]
    zl, core, same = place_ref[0], place_ref[1], place_ref[2]
    channels = part_buf.shape[1] // 2

    def copies(slots, wanted, first, dst, sem):
        out = []
        for d in range(ring):
            todo, row = [], first
            for ref in slots[d]:
                n = ref.shape[0]
                todo.append(pltpu.make_async_copy(ref, dst.at[pl.ds(row, n)], sem))
                row += n
            out.append((d, todo))
        return out

    def slice_at(j):
        return lax.rem(zl + 1 + j, depth)

    for j in range(depth):
        k = slice_at(j)
        own_d = lax.rem(k - zl + ring, ring)
        far_d = lax.rem(k - zl + ring // 2 + ring, ring)
        near_d = lax.rem(k - zl + ring + (1 - same) * (ring // 2), ring)
        first = pl.multiple_of(zl * rows, rows)
        for d in range(ring):
            if d == ring // 2:
                continue

            @pl.when(own_d == d)
            def _():
                pltpu.make_async_copy(
                    own_slots[d][0].at[pl.ds(first, rows)],
                    own_buf.at[j, :, pl.ds(EDGE, length)],
                    own_sem.at[j],
                ).start()

        for slots, wanted, row, sem in (
            (swap_slots, near_d, 0, near_sem),
            (own_slots, far_d, channels, far_sem),
        ):
            for d, todo in copies(slots, wanted, row, part_buf.at[j], sem.at[j]):

                @pl.when(wanted == d)
                def _():
                    for copy in todo:
                        copy.start()

    def body(j, carry):
        k = slice_at(j)
        left, right = k - 1 + core, k + core
        left_ok = (left >= 0).astype(jnp.bfloat16)
        right_ok = (right < depth).astype(jnp.bfloat16)
        left_at = jnp.clip(left - zl + depth - 1, 0, 2 * depth - 2)
        right_at = jnp.clip(right - zl + depth - 1, 0, 2 * depth - 2)
        own_buf[j, :, :EDGE] = edge_ref[left_at, 1] * left_ok
        own_buf[j, :, EDGE + length :] = edge_ref[right_at, 0] * right_ok
        pltpu.make_async_copy(
            own_buf.at[j, :, pl.ds(EDGE, length)],
            own_buf.at[j, :, pl.ds(EDGE, length)],
            own_sem.at[j],
        ).wait()
        half = part_buf.at[j, pl.ds(0, channels)]
        pltpu.make_async_copy(half, half, near_sem.at[j]).wait()
        pltpu.make_async_copy(half, half, far_sem.at[j]).wait()
        partner = part_buf[j]
        for group in range(LAGS // GROUP):
            stacked = jnp.concatenate(
                [
                    own_buf[j, :, EDGE + LAGH - lag : EDGE + LAGH - lag + length]
                    for lag in range(group * GROUP, (group + 1) * GROUP)
                ],
                axis=0,
            )
            block = pl.ds(group * GROUP * rows, GROUP * rows)
            product = lax.dot_general(
                stacked, partner, (((1,), (1,)), ((), ())), preferred_element_type=jnp.float32
            )
            acc[block] = jnp.where(j == 0, product, acc[block] + product)
        return carry

    acc[...] = jnp.zeros_like(acc)
    lax.fori_loop(0, depth, body, 0)
    half_rows = rows // 2

    def spread(lag, carry):
        base = lag * rows
        for ref, which in ((mine_ref, core), (other_ref, 1 - core)):
            start = pl.multiple_of(base + which * half_rows, half_rows)
            for r in range(ROUNDS):
                ref[r, lag] = (
                    acc[pl.ds(start, half_rows), r * channels : (r + 1) * channels] * scale
                )
        return carry

    lax.fori_loop(0, LAGS, spread, 0)


def lagged(layout, own, swapped, edges, place, channels, length, scale):
    rows = channels // layout.depth
    depth = layout.depth
    operands = [ref for slots in (own, swapped) for d in range(layout.ring) for ref in slots[d]]
    shape = jax.ShapeDtypeStruct((ROUNDS, LAGS, rows // 2, channels), jnp.float32)
    return pl.pallas_call(
        functools.partial(lagged_kernel, layout, rows, length, scale),
        out_shape=(shape, shape),
        in_specs=[
            pl.BlockSpec(memory_space=pltpu.SMEM),
            pl.BlockSpec(memory_space=pltpu.VMEM),
        ]
        + [pl.BlockSpec(memory_space=pl.ANY)] * len(operands),
        out_specs=(pl.BlockSpec(memory_space=pltpu.VMEM),) * 2,
        scratch_shapes=[
            pltpu.VMEM((depth, rows, length + 2 * EDGE), jnp.bfloat16),
            pltpu.VMEM((depth, 2 * channels, length), jnp.bfloat16),
            pltpu.VMEM((LAGS * rows, 2 * channels), jnp.float32),
            pltpu.SemaphoreType.DMA((depth,)),
            pltpu.SemaphoreType.DMA((depth,)),
            pltpu.SemaphoreType.DMA((depth,)),
        ],
        compiler_params=pltpu.CompilerParams(vmem_limit_bytes=40 * 1024 * 1024),
        name="lagged",
    )(place, edges, *operands)


def on_device(raw_strain, band_index, filter_taps):
    layout = Layout()
    channels, length = raw_strain.shape
    rows = channels // layout.depth
    scale = 1.0 / math.sqrt(length * layout.slices)
    block = lax.axis_index("ch")
    piece = lax.axis_index("ta")
    zl, core = piece // 2, piece % 2
    same = ((block % layout.cols) >= layout.cols // 2).astype(jnp.int32)
    place = jnp.stack([zl, core, same]).astype(jnp.int32)

    normalized = normalize(raw_strain, band_index, filter_taps)
    swapped_piece = lax.ppermute(normalized, AXES, layout.swap_columns())
    own = gather_ring(layout, normalized)
    swapped = gather_ring(layout, swapped_piece)

    mine = []
    for d in range(1 - layout.depth, layout.depth):
        slot = own[d % layout.ring][0]
        part = lax.dynamic_slice_in_dim(slot, zl * rows, rows, 0)
        mine.append(jnp.stack([part[:, :EDGE], part[:, length - EDGE :]]))
    edges = lax.ppermute(jnp.stack(mine), AXES, layout.swap_cores())

    kept, sent = lagged(layout, own, swapped, edges, place, channels, length, scale)
    return kept + lax.ppermute(sent, AXES, layout.swap_cores())


def solution(mesh):
    placed = (P("ch", "ta"), P("ch"), P())
    return jax.shard_map(
        on_device,
        mesh=mesh,
        in_specs=placed,
        out_specs=P(None, None, ("ch", "ta"), None),
        check_vma=False,
    )
```

```python
import functools
import math

import jax
import jax.numpy as jnp
from jax import lax
from jax.experimental import pallas as pl
from jax.experimental.pallas import tpu as pltpu
from jax.sharding import PartitionSpec as P

HF = 16
TAPS = 33
NBANDS = 4
LAGH = 32
LAGS = 65
ROUNDS = 2
EDGE = 128
PAIRS = LAGH + 1
GROUP = 11
AXES = ("ch", "ta")


class Layout:
    def __init__(self):
        self.blocks = lax.axis_size("ch")
        self.slices = lax.axis_size("ta")
        self.cols = self.blocks // 2
        self.depth = self.slices // 2
        self.ring = 2 * self.depth

    def index(self, pos, col, core):
        zh, zl = divmod(pos % self.ring, self.depth)
        return (zh * self.cols + col) * self.slices + zl * 2 + core

    def every(self):
        for pos in range(self.ring):
            for col in range(self.cols):
                for core in range(2):
                    yield pos, col, core

    def from_ring(self, step):
        return [(self.index(p + step, c, k), self.index(p, c, k)) for p, c, k in self.every()]

    def swap_columns(self):
        return [
            (self.index(p, (c + self.cols // 2) % self.cols, k), self.index(p, c, k))
            for p, c, k in self.every()
        ]

    def swap_cores(self):
        return [(self.index(p, c, 1 - k), self.index(p, c, k)) for p, c, k in self.every()]


def to_neighbours(low_part, high_part):
    count = lax.axis_size("ta")
    forward = [(i, i + 1) for i in range(count - 1)]
    backward = [(i + 1, i) for i in range(count - 1)]
    from_low = lax.ppermute(high_part, "ta", forward)
    from_high = lax.ppermute(low_part, "ta", backward)
    return from_low, from_high


def normalize(raw, band_index, filter_taps):
    length = raw.shape[1]
    time_groups = lax.axis_size("ta")
    whole_len = length * time_groups
    onehot = (band_index[:, None] == jnp.arange(NBANDS, dtype=jnp.int32)[None, :]).astype(
        jnp.float32
    )
    coeffs = jnp.dot(
        onehot, filter_taps, precision=lax.Precision.HIGHEST, preferred_element_type=jnp.float32
    )
    low, high = to_neighbours(raw[:, :HF], raw[:, length - HF :])
    extended = jnp.concatenate([low, raw, high], axis=1)
    filtered = jnp.zeros_like(raw)
    for step in range(TAPS):
        filtered = filtered + coeffs[:, step : step + 1] * extended[:, step : step + length]
    magnitude = jnp.abs(filtered)
    prefix = jnp.cumsum(magnitude, axis=1)
    total = prefix[:, length - 1 :]
    suffix = total - prefix + magnitude
    before, after = to_neighbours(prefix, suffix)
    window_sum = before + total + after
    global_time = lax.axis_index("ta") * length + jnp.arange(length, dtype=jnp.int32)
    upper = jnp.minimum(global_time + length, whole_len - 1) + 1
    lower = jnp.maximum(global_time - length, 0)
    counted = (upper - lower).astype(jnp.float32)
    level = window_sum / counted[None, :]
    return (filtered / (level + 1e-06)).astype(jnp.bfloat16)


def gather_ring(layout, piece):
    ring = layout.ring
    slots = {0: (piece,)}
    up = down = piece
    for step in range(1, ring // 2):
        up = lax.ppermute(up, AXES, layout.from_ring(1))
        down = lax.ppermute(down, AXES, layout.from_ring(-1))
        slots[step] = (up,)
        slots[ring - step] = (down,)
    half = piece.shape[0] // 2
    slots[ring // 2] = (
        lax.ppermute(up[:half], AXES, layout.from_ring(1)),
        lax.ppermute(down[half:], AXES, layout.from_ring(-1)),
    )
    return slots


class Job:
    def __init__(self, ring, steps, slots_of_rows, first_edge, last):
        self.ring = ring
        self.depth = ring // 2
        self.steps = steps
        self.slots_of_rows = slots_of_rows
        self.first_edge = first_edge
        self.last = last

    def row_slots(self):
        return sorted({s % self.ring for d in self.steps for s in (d, d - self.depth)} - {self.depth})

    def partner_slots(self):
        return sorted({(s + f) % self.ring for d in self.steps for s in (d, d - self.depth)
                       for f in (0, self.depth)})


def lagged_kernel(job, rows, length, scale, n_rows, partner_counts, has_acc, *refs):
    refs = list(refs)
    place_ref, edge_ref = refs.pop(0), refs.pop(0)
    row_refs = [refs.pop(0) for _ in range(n_rows)]
    partner_refs = {d: [refs.pop(0) for _ in range(n)] for d, n in partner_counts.items()}
    acc_in = refs.pop(0) if has_acc else None
    if job.last:
        mine_ref, other_ref, own_buf, part_buf, both_buf, row_sem, part_sem, acc = refs
    else:
        acc, own_buf, part_buf, both_buf, row_sem, part_sem = refs
    ring, depth = job.ring, job.depth
    zl, core, far = place_ref[0], place_ref[1], place_ref[2]
    channels = part_buf.shape[1]
    count = len(job.steps)
    first_step = job.steps[0]
    deep = length + EDGE

    for j, step in enumerate(job.steps):
        k = lax.rem(zl + step, depth)
        target = own_buf.at[j, :, pl.ds(EDGE, length)]
        if job.slots_of_rows:
            own_d = lax.rem(k - zl + ring, ring)
            first = pl.multiple_of(zl * rows, rows)
            for d, ref in zip(job.row_slots(), row_refs, strict=True):

                @pl.when(own_d == d)
                def _():
                    pltpu.make_async_copy(
                        ref.at[pl.ds(first, rows)], target, row_sem.at[j]
                    ).start()

        else:
            pltpu.make_async_copy(row_refs[0].at[k], target, row_sem.at[j]).start()
        wanted = lax.rem(k - zl + ring + far * depth, ring)
        for d, halves in partner_refs.items():

            @pl.when(wanted == d)
            def _():
                row = 0
                for ref in halves:
                    n = ref.shape[0]
                    pltpu.make_async_copy(
                        ref, part_buf.at[j, pl.ds(row, n), pl.ds(EDGE, length)], part_sem.at[j]
                    ).start()
                    row += n

    if has_acc:
        acc[...] = acc_in[...]
    else:
        acc[...] = jnp.zeros_like(acc)
    for j in range(count):
        own_buf[j, :, deep + EDGE :] = jnp.zeros((rows, EDGE), jnp.bfloat16)
        part_buf[j, :, :EDGE] = jnp.zeros((channels, EDGE), jnp.bfloat16)
        part_buf[j, :, deep:] = jnp.zeros((channels, EDGE), jnp.bfloat16)

    def body(j, carry):
        k = lax.rem(zl + first_step + j, depth)
        left, right = k - 1 + core, k + core
        left_ok = (left >= 0).astype(jnp.bfloat16)
        right_ok = (right < depth).astype(jnp.bfloat16)
        base = job.first_edge - zl if job.slots_of_rows else job.first_edge
        left_at = base + jnp.maximum(left, 0)
        right_at = base + jnp.minimum(right, depth - 1)
        own_buf[j, :, :EDGE] = edge_ref[left_at, 1] * left_ok
        own_buf[j, :, deep : deep + EDGE] = edge_ref[right_at, 0] * right_ok
        for buf, sem in ((own_buf, row_sem), (part_buf, part_sem)):
            whole = buf.at[j, :, pl.ds(EDGE, length)]
            pltpu.make_async_copy(whole, whole, sem.at[j]).wait()
        both_buf[:channels] = part_buf[j, :, EDGE : EDGE + deep]
        both_buf[channels:] = part_buf[j, :, EDGE - 1 : EDGE - 1 + deep]
        partner = both_buf[...]
        for group in range(PAIRS // GROUP):
            stacked = jnp.concatenate(
                [
                    own_buf[j, :, EDGE + LAGH - 2 * a : EDGE + LAGH - 2 * a + deep]
                    for a in range(group * GROUP, (group + 1) * GROUP)
                ],
                axis=0,
            )
            block = pl.ds(group * GROUP * rows, GROUP * rows)
            acc[block] += lax.dot_general(
                stacked, partner, (((1,), (1,)), ((), ())), preferred_element_type=jnp.float32
            )
        return carry

    lax.fori_loop(0, count, body, 0)
    if not job.last:
        return
    half_rows = rows // 2

    for ref, which in ((mine_ref, core), (other_ref, 1 - core)):
        for a in range(PAIRS):
            start = pl.multiple_of(a * rows + which * half_rows, half_rows)
            ref[2 * a] = acc[pl.ds(start, half_rows), :channels] * scale
            if a > 0:
                ref[2 * a - 1] = acc[pl.ds(start, half_rows), channels:] * scale


def lagged(job, place, edges, row_arrays, slots, rows, scale, acc=None):
    channels, length = slots[0][0].shape
    if job.slots_of_rows:
        row_arrays = [slots[d][0] for d in job.row_slots()]
    partners = {d: slots[d] for d in job.partner_slots()}
    operands = list(row_arrays) + [ref for d in partners for ref in partners[d]]
    count = len(job.steps)
    half = jax.ShapeDtypeStruct((LAGS, rows // 2, channels), jnp.float32)
    full = (PAIRS * rows, 2 * channels)
    vmem = pl.BlockSpec(memory_space=pltpu.VMEM)
    scratch = [
        pltpu.VMEM((count, rows, length + 3 * EDGE), jnp.bfloat16),
        pltpu.VMEM((count, channels, length + 2 * EDGE), jnp.bfloat16),
        pltpu.VMEM((2 * channels, length + EDGE), jnp.bfloat16),
        pltpu.SemaphoreType.DMA((count,)),
        pltpu.SemaphoreType.DMA((count,)),
    ]
    if job.last:
        scratch.append(pltpu.VMEM(full, jnp.float32))
    has_acc = acc is not None
    return pl.pallas_call(
        functools.partial(
            lagged_kernel,
            job,
            rows,
            length,
            scale,
            len(row_arrays),
            {d: len(p) for d, p in partners.items()},
            has_acc,
        ),
        out_shape=(half, half) if job.last else jax.ShapeDtypeStruct(full, jnp.float32),
        in_specs=[pl.BlockSpec(memory_space=pltpu.SMEM), vmem]
        + [pl.BlockSpec(memory_space=pl.ANY)] * len(operands)
        + [vmem] * has_acc,
        out_specs=(vmem, vmem) if job.last else vmem,
        scratch_shapes=scratch,
        compiler_params=pltpu.CompilerParams(vmem_limit_bytes=32 * 1024 * 1024),
        cost_estimate=pl.CostEstimate(
            flops=2 * count * full[0] * full[1] * length,
            bytes_accessed=2 * count * channels * length,
            transcendentals=0,
        ),
        name="lagged",
    )(place, edges, *operands, *([acc] if has_acc else []))


def on_device(raw_strain, band_index, filter_taps):
    layout = Layout()
    channels, length = raw_strain.shape
    depth, ring = layout.depth, layout.ring
    rows = channels // depth
    scale = 1.0 / math.sqrt(length * layout.slices)
    block = lax.axis_index("ch")
    piece = lax.axis_index("ta")
    zl, core = piece // 2, piece % 2
    upper = ((block % layout.cols) >= layout.cols // 2).astype(jnp.int32)
    place0 = jnp.stack([zl, core, upper]).astype(jnp.int32)
    place1 = jnp.stack([zl, core, jnp.int32(1)]).astype(jnp.int32)

    normalized = normalize(raw_strain, band_index, filter_taps)
    swapped = lax.ppermute(normalized, AXES, layout.swap_columns())
    slots = gather_ring(layout, normalized)
    groups = [[2 * z + c for z in range(depth)] for c in range(2)]
    guest_rows = lax.all_to_all(
        swapped.reshape(depth, rows, length), "ta", 0, 0, axis_index_groups=groups
    )

    mine = []
    for d in range(1 - depth, depth):
        part = lax.dynamic_slice_in_dim(slots[d % ring][0], zl * rows, rows, 0)
        mine.append(jnp.stack([part[:, :EDGE], part[:, length - EDGE :]]))
    guest_edges = jnp.stack([guest_rows[:, :, :EDGE], guest_rows[:, :, length - EDGE :]], axis=1)
    edges = lax.ppermute(
        jnp.concatenate([jnp.stack(mine), guest_edges], axis=0), AXES, layout.swap_cores()
    )

    guest = 2 * depth - 1
    early = Job(ring, tuple(range(1, depth)), False, guest, False)
    late = Job(ring, (0,), False, guest, True)
    own = Job(ring, tuple(range(1, depth + 1)), True, depth - 1, True)
    acc = lagged(early, place0, edges, [guest_rows], slots, rows, scale)
    kept, sent = lagged(late, place0, edges, [guest_rows], slots, rows, scale, acc)
    result = kept + lax.ppermute(sent, AXES, layout.swap_cores())
    first = lax.ppermute(result, AXES, layout.swap_columns())
    kept, sent = lagged(own, place1, edges, [], slots, rows, scale)
    second = kept + lax.ppermute(sent, AXES, layout.swap_cores())
    return jnp.stack([first, second])


def solution(mesh):
    placed = (P("ch", "ta"), P("ch"), P())
    return jax.shard_map(
        on_device,
        mesh=mesh,
        in_specs=placed,
        out_specs=P(None, None, ("ch", "ta"), None),
        check_vma=False,
    )
```

```python
import functools
import math

import jax
import jax.numpy as jnp
from jax import lax
from jax.experimental import pallas as pl
from jax.experimental.pallas import tpu as pltpu
from jax.sharding import Mesh
from jax.sharding import PartitionSpec as P

HF = 16
TAPS = 33
NBANDS = 4
LAGH = 32
LAGS = 65
PAIRS = LAGH + 1
LANES = 128
CHUNK = 64


def to_neighbours(low_part, high_part):
    count = lax.axis_size("ta")
    forward = [(i, i + 1) for i in range(count - 1)]
    backward = [(i + 1, i) for i in range(count - 1)]
    from_low = lax.ppermute(high_part, "ta", forward)
    from_high = lax.ppermute(low_part, "ta", backward)
    return from_low, from_high


def filter_kernel(
    taps_ref, band_ref, raw_ref, low_ref, high_ref, out_ref, prefix_ref, suffix_ref, tall, wide, coeff
):
    channels, length = raw_ref.shape
    tiles = length // LANES
    tall[:HF] = low_ref[...]
    tall[HF + length :] = high_ref[...]
    for i in range(tiles):
        tall[HF + i * LANES : HF + (i + 1) * LANES] = raw_ref[:, i * LANES : (i + 1) * LANES].T
    band = jnp.broadcast_to(band_ref[...], (8, channels))
    for k in range(TAPS):
        value = jnp.full((8, channels), taps_ref[NBANDS - 1, k])
        for b in range(NBANDS - 1):
            value = jnp.where(band == b, taps_ref[b, k], value)
        coeff[k] = value

    def chunk(i, carry):
        base = pl.multiple_of(i * CHUNK, CHUNK)
        total = jnp.zeros((CHUNK, channels), jnp.float32)
        for k in range(TAPS):
            factor = jnp.broadcast_to(coeff[k][None], (CHUNK // 8, 8, channels))
            total = total + factor.reshape(CHUNK, channels) * tall[pl.ds(base + k, CHUNK), :]
        wide[pl.ds(base, CHUNK), :] = total
        return carry

    lax.fori_loop(0, length // CHUNK, chunk, 0)
    inner = jnp.zeros((channels, LANES), jnp.float32)
    for r in range(tiles):
        piece = wide[pl.ds(r, LANES, stride=tiles), :].T
        cols = slice(r * LANES, (r + 1) * LANES)
        out_ref[:, cols] = piece
        inner = inner + jnp.abs(piece)
        prefix_ref[:, cols] = inner
    row = lax.broadcasted_iota(jnp.int32, (LANES, LANES), 0)
    col = lax.broadcasted_iota(jnp.int32, (LANES, LANES), 1)
    before = jnp.dot(
        inner,
        (row < col).astype(jnp.float32),
        precision=lax.Precision.HIGHEST,
        preferred_element_type=jnp.float32,
    )
    total = (before + inner)[:, LANES - 1 :]
    for r in range(tiles):
        cols = slice(r * LANES, (r + 1) * LANES)
        prefix = prefix_ref[:, cols] + before
        prefix_ref[:, cols] = prefix
        suffix_ref[:, cols] = (total - prefix) + jnp.abs(out_ref[:, cols])


def filtered_sums(raw, band_index, filter_taps):
    channels, length = raw.shape
    low, high = to_neighbours(raw[:, :HF].T, raw[:, length - HF :].T)
    shape = jax.ShapeDtypeStruct((channels, length), jnp.float32)
    vmem = pl.BlockSpec(memory_space=pltpu.VMEM)
    return pl.pallas_call(
        filter_kernel,
        out_shape=(shape,) * 3,
        in_specs=[pl.BlockSpec(memory_space=pltpu.SMEM)] + [vmem] * 4,
        out_specs=(vmem,) * 3,
        scratch_shapes=[
            pltpu.VMEM((length + 2 * HF, channels), jnp.float32),
            pltpu.VMEM((length, channels), jnp.float32),
            pltpu.VMEM((TAPS, 8, channels), jnp.float32),
        ],
        compiler_params=pltpu.CompilerParams(vmem_limit_bytes=24 * 1024 * 1024),
        name="filter",
    )(filter_taps, band_index[None, :], raw, low, high)


def normalize(raw, band_index, filter_taps):
    channels, length = raw.shape
    tiles = length // LANES
    whole_len = length * lax.axis_size("ta")
    filtered, prefix, suffix = filtered_sums(raw, band_index, filter_taps)
    before, after = to_neighbours(prefix, suffix)
    window_sum = before + prefix[:, length - 1 :] + after
    at = jnp.arange(length, dtype=jnp.int32)
    local_time = tiles * (at % LANES) + at // LANES
    global_time = lax.axis_index("ta") * length + local_time
    upper = jnp.minimum(global_time + length, whole_len - 1) + 1
    lower = jnp.maximum(global_time - length, 0)
    counted = (upper - lower).astype(jnp.float32)
    level = window_sum / counted[None, :]
    return (filtered / (level + 1e-06)).astype(jnp.bfloat16)


def lagged_kernel(
    count, scale, place_ref, own_ref, left_ref, right_ref, part_ref, out_ref, fan, both, carry, acc
):
    step = pl.program_id(0)
    rows = own_ref.shape[1]
    channels, length = part_ref.shape[1:]
    tiles = length // LANES
    reach = -(-LAGH // tiles)
    lead = reach * tiles + LAGH

    @pl.when(step == 0)
    def _():
        acc[...] = jnp.zeros_like(acc)
        carry[...] = jnp.zeros_like(carry)

    lane = lax.broadcasted_iota(jnp.int32, (rows, length), 1) % LANES
    inside = own_ref[0].astype(jnp.float32)
    left = jnp.where(step > 0, left_ref[0].astype(jnp.float32), 0.0)
    right = jnp.where(step < count - 1, right_ref[0].astype(jnp.float32), 0.0)
    for j in range(-reach, reach + 1):
        if j < 0:
            mixed = jnp.where(lane >= LANES + j, left, inside)
        else:
            mixed = jnp.where(lane < j, right, inside)
        for r in range(tiles):
            tile = mixed[:, r * LANES : (r + 1) * LANES]
            if j != 0:
                tile = pltpu.roll(tile, (-j) % LANES, 1)
            at = (j + reach) * tiles + r
            fan[:, at * LANES : (at + 1) * LANES] = tile.astype(jnp.bfloat16)

    both[:channels] = part_ref[0]
    both[channels:, LANES:] = part_ref[0, :, : length - LANES]
    final = part_ref[0, :, length - LANES :].astype(jnp.float32)
    part_lane = lax.broadcasted_iota(jnp.int32, (channels, LANES), 1)
    late = pltpu.roll(jnp.where(part_lane == LANES - 1, carry[...], final), 1, 1)
    both[channels:, :LANES] = late.astype(jnp.bfloat16)
    carry[...] = final

    def moved(width, offset):
        return jnp.concatenate(
            [
                fan[:, (lead - 2 * a + offset) * LANES : (lead - 2 * a + offset + width) * LANES]
                for a in range(PAIRS)
            ],
            axis=0,
        )

    acc[...] += lax.dot_general(
        moved(tiles, 0), both[...], (((1,), (1,)), ((), ())), preferred_element_type=jnp.float32
    )

    @pl.when(step == count - 1)
    def _():
        tail = jnp.where(part_lane == LANES - 1, final, 0.0).astype(jnp.bfloat16)
        acc[:, channels:] += lax.dot_general(
            moved(1, tiles), tail, (((1,), (1,)), ((), ())), preferred_element_type=jnp.float32
        )
        for a in range(PAIRS):
            block = acc[a * rows : (a + 1) * rows] * scale
            out_ref[2 * a] = block[:, :channels].astype(out_ref.dtype)
            if a > 0:
                out_ref[2 * a - 1] = block[:, channels:].astype(out_ref.dtype)


def lagged(place, own_rows, partner, rows, count, scale, out_dtype=jnp.float32):
    channels, length = partner.shape[1:]
    tiles = length // LANES
    fan_tiles = (2 * -(-LAGH // tiles) + 1) * tiles
    row_block = (1, rows, length)
    spec = pltpu.PrefetchScalarGridSpec(
        num_scalar_prefetch=1,
        grid=(count,),
        in_specs=[
            pl.BlockSpec(row_block, lambda t, p: (p[0] + t, p[1], 0)),
            pl.BlockSpec(row_block, lambda t, p: (p[0] + jnp.maximum(t - 1, 0), p[1], 0)),
            pl.BlockSpec(row_block, lambda t, p: (p[0] + jnp.minimum(t + 1, count - 1), p[1], 0)),
            pl.BlockSpec((1, channels, length), lambda t, p: (p[2] + t, 0, 0)),
        ],
        out_specs=pl.BlockSpec((LAGS, rows, channels), lambda t, p: (0, 0, 0)),
        scratch_shapes=[
            pltpu.VMEM((rows, fan_tiles * LANES), jnp.bfloat16),
            pltpu.VMEM((2 * channels, length), jnp.bfloat16),
            pltpu.VMEM((channels, LANES), jnp.float32),
            pltpu.VMEM((PAIRS * rows, 2 * channels), jnp.float32),
        ],
    )
    return pl.pallas_call(
        functools.partial(lagged_kernel, count, scale),
        out_shape=jax.ShapeDtypeStruct((LAGS, rows, channels), out_dtype),
        grid_spec=spec,
        compiler_params=pltpu.CompilerParams(vmem_limit_bytes=24 * 1024 * 1024),
        cost_estimate=pl.CostEstimate(
            flops=4 * count * PAIRS * rows * channels * length,
            bytes_accessed=2 * count * channels * length,
            transcendentals=0,
        ),
        name="lagged",
    )(place, own_rows, own_rows, own_rows, partner)


def on_device(raw_strain, band_index, filter_taps):
    channels, length = raw_strain.shape
    count = lax.axis_size("ta")
    rows = channels // count
    scale = 1.0 / math.sqrt(length * count)
    swap = [(0, 1), (1, 0)]
    half, upper, piece = lax.axis_index("zh"), lax.axis_index("cp"), lax.axis_index("ta")

    normalized = normalize(raw_strain, band_index, filter_taps)
    ring = lax.all_gather(normalized, ("zh", "ta"), axis=0, tiled=False)
    guest = lax.ppermute(normalized, "cp", swap)
    guest = lax.all_to_all(guest.reshape(count, rows, length), "ta", 0, 0)

    other = (1 - half) * count
    near = jnp.where(upper == 1, other, half * count)
    place0 = jnp.stack([0 * piece, 0 * piece, near]).astype(jnp.int32)
    place1 = jnp.stack([half * count, piece, other]).astype(jnp.int32)
    first = lagged(place0, guest, ring, rows, count, scale)
    first = lax.ppermute(first, "cp", swap)
    second = lagged(place1, ring, ring, rows, count, scale)
    return jnp.stack([first, second])


def solution(mesh):
    blocks, slices = mesh.devices.shape
    axes = ("zh", "cp", "col", "ta")
    parts = Mesh(mesh.devices.reshape(2, 2, blocks // 4, slices), axes)
    channel_axes = axes[:3]
    return jax.shard_map(
        on_device,
        mesh=parts,
        in_specs=(P(channel_axes, "ta"), P(channel_axes), P()),
        out_specs=P(None, None, axes, None),
        check_vma=False,
    )
```

```python
import functools
import math

import jax
import jax.numpy as jnp
from jax import lax
from jax.experimental import pallas as pl
from jax.experimental.pallas import tpu as pltpu
from jax.sharding import Mesh
from jax.sharding import PartitionSpec as P

HF = 16
TAPS = 33
NBANDS = 4
LAGH = 32
LAGS = 65
PAIRS = LAGH + 1
LANES = 128
CHUNK = 64
VMEM_BYTES = 58 * 1024 * 1024


def to_neighbours(low_part, high_part):
    count = lax.axis_size("ta")
    forward = [(i, i + 1) for i in range(count - 1)]
    backward = [(i + 1, i) for i in range(count - 1)]
    from_low = lax.ppermute(high_part, "ta", forward)
    from_high = lax.ppermute(low_part, "ta", backward)
    return from_low, from_high


def filter_kernel(
    taps_ref, band_ref, raw_ref, low_ref, high_ref, out_ref, prefix_ref, suffix_ref, tall, wide, coeff
):
    channels, length = raw_ref.shape
    tiles = length // LANES
    tall[:HF] = low_ref[...]
    tall[HF + length :] = high_ref[...]
    for i in range(tiles):
        tall[HF + i * LANES : HF + (i + 1) * LANES] = raw_ref[:, i * LANES : (i + 1) * LANES].T
    band = jnp.broadcast_to(band_ref[...], (8, channels))
    for k in range(TAPS):
        value = jnp.full((8, channels), taps_ref[NBANDS - 1, k])
        for b in range(NBANDS - 1):
            value = jnp.where(band == b, taps_ref[b, k], value)
        coeff[k] = value

    def chunk(i, carry):
        base = pl.multiple_of(i * CHUNK, CHUNK)
        total = jnp.zeros((CHUNK, channels), jnp.float32)
        for k in range(TAPS):
            factor = jnp.broadcast_to(coeff[k][None], (CHUNK // 8, 8, channels))
            total = total + factor.reshape(CHUNK, channels) * tall[pl.ds(base + k, CHUNK), :]
        wide[pl.ds(base, CHUNK), :] = total
        return carry

    lax.fori_loop(0, length // CHUNK, chunk, 0)
    inner = jnp.zeros((channels, LANES), jnp.float32)
    for r in range(tiles):
        piece = wide[pl.ds(r, LANES, stride=tiles), :].T
        cols = slice(r * LANES, (r + 1) * LANES)
        out_ref[:, cols] = piece
        inner = inner + jnp.abs(piece)
        prefix_ref[:, cols] = inner
    row = lax.broadcasted_iota(jnp.int32, (LANES, LANES), 0)
    col = lax.broadcasted_iota(jnp.int32, (LANES, LANES), 1)
    before = jnp.dot(
        inner,
        (row < col).astype(jnp.float32),
        precision=lax.Precision.HIGHEST,
        preferred_element_type=jnp.float32,
    )
    total = (before + inner)[:, LANES - 1 :]
    for r in range(tiles):
        cols = slice(r * LANES, (r + 1) * LANES)
        prefix = prefix_ref[:, cols] + before
        prefix_ref[:, cols] = prefix
        suffix_ref[:, cols] = (total - prefix) + jnp.abs(out_ref[:, cols])


def filtered_sums(raw, band_index, filter_taps):
    channels, length = raw.shape
    low, high = to_neighbours(raw[:, :HF].T, raw[:, length - HF :].T)
    shape = jax.ShapeDtypeStruct((channels, length), jnp.float32)
    vmem = pl.BlockSpec(memory_space=pltpu.VMEM)
    return pl.pallas_call(
        filter_kernel,
        out_shape=(shape,) * 3,
        in_specs=[pl.BlockSpec(memory_space=pltpu.SMEM)] + [vmem] * 4,
        out_specs=(vmem,) * 3,
        scratch_shapes=[
            pltpu.VMEM((length + 2 * HF, channels), jnp.float32),
            pltpu.VMEM((length, channels), jnp.float32),
            pltpu.VMEM((TAPS, 8, channels), jnp.float32),
        ],
        compiler_params=pltpu.CompilerParams(vmem_limit_bytes=24 * 1024 * 1024),
        name="filter",
    )(filter_taps, band_index[None, :], raw, low, high)


def normalize(raw, band_index, filter_taps):
    channels, length = raw.shape
    tiles = length // LANES
    whole_len = length * lax.axis_size("ta")
    filtered, prefix, suffix = filtered_sums(raw, band_index, filter_taps)
    before, after = to_neighbours(prefix, suffix)
    window_sum = before + prefix[:, length - 1 :] + after
    at = jnp.arange(length, dtype=jnp.int32)
    local_time = tiles * (at % LANES) + at // LANES
    global_time = lax.axis_index("ta") * length + local_time
    upper = jnp.minimum(global_time + length, whole_len - 1) + 1
    lower = jnp.maximum(global_time - length, 0)
    counted = (upper - lower).astype(jnp.float32)
    level = window_sum / counted[None, :]
    return (filtered / (level + 1e-06)).astype(jnp.bfloat16)


def lagged_kernel(
    count, scale, place_ref, own_ref, left_ref, right_ref, part_ref, out_ref, fan, both, carry, acc
):
    step = pl.program_id(0)
    rows = own_ref.shape[1]
    channels, length = part_ref.shape[1:]
    tiles = length // LANES
    reach = -(-LAGH // tiles)
    lead = reach * tiles + LAGH

    @pl.when(step == 0)
    def _():
        acc[...] = jnp.zeros_like(acc)
        carry[...] = jnp.zeros_like(carry)

    lane = lax.broadcasted_iota(jnp.int32, (rows, length), 1) % LANES
    inside = own_ref[0].astype(jnp.float32)
    left = jnp.where(step > 0, left_ref[0].astype(jnp.float32), 0.0)
    right = jnp.where(step < count - 1, right_ref[0].astype(jnp.float32), 0.0)
    for j in range(-reach, reach + 1):
        if j < 0:
            mixed = jnp.where(lane >= LANES + j, left, inside)
        else:
            mixed = jnp.where(lane < j, right, inside)
        for r in range(tiles):
            tile = mixed[:, r * LANES : (r + 1) * LANES]
            if j != 0:
                tile = pltpu.roll(tile, (-j) % LANES, 1)
            at = (j + reach) * tiles + r
            fan[:, at * LANES : (at + 1) * LANES] = tile.astype(jnp.bfloat16)

    both[:channels] = part_ref[0]
    both[channels:, LANES:] = part_ref[0, :, : length - LANES]
    final = part_ref[0, :, length - LANES :].astype(jnp.float32)
    part_lane = lax.broadcasted_iota(jnp.int32, (channels, LANES), 1)
    late = pltpu.roll(jnp.where(part_lane == LANES - 1, carry[...], final), 1, 1)
    both[channels:, :LANES] = late.astype(jnp.bfloat16)
    carry[...] = final

    def moved(width, offset):
        return jnp.concatenate(
            [
                fan[:, (lead - 2 * a + offset) * LANES : (lead - 2 * a + offset + width) * LANES]
                for a in range(PAIRS)
            ],
            axis=0,
        )

    acc[...] += lax.dot_general(
        moved(tiles, 0), both[...], (((1,), (1,)), ((), ())), preferred_element_type=jnp.float32
    )

    @pl.when(step == count - 1)
    def _():
        tail = jnp.where(part_lane == LANES - 1, final, 0.0).astype(jnp.bfloat16)
        acc[:, channels:] += lax.dot_general(
            moved(1, tiles), tail, (((1,), (1,)), ((), ())), preferred_element_type=jnp.float32
        )
        for a in range(PAIRS):
            block = acc[a * rows : (a + 1) * rows] * scale
            out_ref[2 * a] = block[:, :channels].astype(out_ref.dtype)
            if a > 0:
                out_ref[2 * a - 1] = block[:, channels:].astype(out_ref.dtype)


def lagged(place, own_rows, partner, rows, count, scale, out_dtype=jnp.float32):
    channels, length = partner.shape[1:]
    tiles = length // LANES
    fan_tiles = (2 * -(-LAGH // tiles) + 1) * tiles
    row_block = (1, rows, length)
    spec = pltpu.PrefetchScalarGridSpec(
        num_scalar_prefetch=1,
        grid=(count,),
        in_specs=[
            pl.BlockSpec(row_block, lambda t, p: (p[0] + t, p[1], 0)),
            pl.BlockSpec(row_block, lambda t, p: (p[0] + jnp.maximum(t - 1, 0), p[1], 0)),
            pl.BlockSpec(row_block, lambda t, p: (p[0] + jnp.minimum(t + 1, count - 1), p[1], 0)),
            pl.BlockSpec((1, channels, length), lambda t, p: (p[2] + t, 0, 0)),
        ],
        out_specs=pl.BlockSpec((LAGS, rows, channels), lambda t, p: (0, 0, 0)),
        scratch_shapes=[
            pltpu.VMEM((rows, fan_tiles * LANES), jnp.bfloat16),
            pltpu.VMEM((2 * channels, length), jnp.bfloat16),
            pltpu.VMEM((channels, LANES), jnp.float32),
            pltpu.VMEM((PAIRS * rows, 2 * channels), jnp.float32),
        ],
    )
    return pl.pallas_call(
        functools.partial(lagged_kernel, count, scale),
        out_shape=jax.ShapeDtypeStruct((LAGS, rows, channels), out_dtype),
        grid_spec=spec,
        compiler_params=pltpu.CompilerParams(vmem_limit_bytes=VMEM_BYTES),
        cost_estimate=pl.CostEstimate(
            flops=4 * count * PAIRS * rows * channels * length,
            bytes_accessed=2 * count * channels * length,
            transcendentals=0,
        ),
        name="lagged",
    )(place, own_rows, own_rows, own_rows, partner)


def on_device(raw_strain, band_index, filter_taps):
    channels, length = raw_strain.shape
    count = lax.axis_size("ta")
    rows = channels // count
    scale = 1.0 / math.sqrt(length * count)
    swap = [(0, 1), (1, 0)]
    half, upper, piece = lax.axis_index("zh"), lax.axis_index("cp"), lax.axis_index("ta")

    normalized = normalize(raw_strain, band_index, filter_taps)
    ring = lax.all_gather(normalized, ("zh", "ta"), axis=0, tiled=False)
    guest = lax.all_to_all(normalized.reshape(count, rows, length), "ta", 0, 0)
    guest = lax.ppermute(guest, "cp", swap)

    other = (1 - half) * count
    near = jnp.where(upper == 1, other, half * count)
    place0 = jnp.stack([0 * piece, 0 * piece, near]).astype(jnp.int32)
    place1 = jnp.stack([half * count, piece, other]).astype(jnp.int32)
    first = lagged(place0, guest, ring, rows, count, scale, jnp.bfloat16)
    first = lax.ppermute(first, "cp", swap)
    second = lagged(place1, ring, ring, rows, count, scale)
    return jnp.stack([first.astype(jnp.float32), second])


def solution(mesh):
    blocks, slices = mesh.devices.shape
    axes = ("zh", "cp", "col", "ta")
    parts = Mesh(mesh.devices.reshape(2, 2, blocks // 4, slices), axes)
    channel_axes = axes[:3]
    return jax.shard_map(
        on_device,
        mesh=parts,
        in_specs=(P(channel_axes, "ta"), P(channel_axes), P()),
        out_specs=P(None, None, axes, None),
        check_vma=False,
    )
```

```python
import functools
import math

import jax
import jax.numpy as jnp
from jax import lax
from jax.experimental import pallas as pl
from jax.experimental.pallas import tpu as pltpu
from jax.sharding import Mesh
from jax.sharding import PartitionSpec as P

HF = 16
TAPS = 33
NBANDS = 4
LAGH = 32
LAGS = 65
PAIRS = LAGH + 1
LANES = 128
AHEAD = 3
ROUNDS = 2
CHUNK = 64
VMEM_BYTES = 58 * 1024 * 1024


def to_neighbours(on_chip, off_chip):
    count = lax.axis_size("ta")
    inner = [(i, i ^ 1) for i in range(count)]
    outer = [(i, i - 1 + 2 * (i % 2)) for i in range(1, count - 1)]
    off_chip = lax.ppermute(off_chip, "ta", outer)
    return lax.ppermute(on_chip, "ta", inner), off_chip


def filter_kernel(
    place_ref, coeff_ref, tall_ref, inner_ref, outer_ref, out_ref, total_ref, on_chip_ref, off_chip_ref, tall, wide
):
    length, channels = tall_ref.shape
    tiles = length // LANES
    first_core = place_ref[1] == 0
    tall[:HF] = jnp.where(first_core, outer_ref[...], inner_ref[...])
    tall[HF : HF + length] = tall_ref[...]
    tall[HF + length :] = jnp.where(first_core, inner_ref[...], outer_ref[...])

    def chunk(i, carry):
        base = pl.multiple_of(i * CHUNK, CHUNK)
        total = jnp.zeros((CHUNK, channels), jnp.float32)
        for k in range(TAPS):
            total = total + coeff_ref[k : k + 1, :] * tall[pl.ds(base + k, CHUNK), :]
        wide[pl.ds(base, CHUNK), :] = total
        return carry

    lax.fori_loop(0, length // CHUNK, chunk, 0)
    lane_total = jnp.zeros((channels, LANES), jnp.float32)
    for r in range(tiles):
        piece = wide[pl.ds(r, LANES, stride=tiles), :].T
        out_ref[:, r * LANES : (r + 1) * LANES] = piece
        lane_total = lane_total + jnp.abs(piece)
    row = lax.broadcasted_iota(jnp.int32, (LANES, LANES), 0)
    col = lax.broadcasted_iota(jnp.int32, (LANES, LANES), 1)
    earlier = jnp.dot(
        lane_total,
        (row < col).astype(jnp.float32),
        precision=lax.Precision.HIGHEST,
        preferred_element_type=jnp.float32,
    )
    total = jnp.broadcast_to((earlier + lane_total)[:, LANES - 1 :], (channels, LANES))
    total_ref[...] = total

    def pack(ref, lanes_sum, order):
        inner = jnp.zeros((channels, LANES), jnp.float32)
        for r in order:
            cols = slice(r * LANES, (r + 1) * LANES)
            inner = inner + jnp.abs(out_ref[:, cols])
            ref[:, cols] = inner.astype(jnp.bfloat16)
        rest = lanes_sum
        for i in range(3):
            term = rest.astype(jnp.bfloat16)
            ref[:, length + i * LANES : length + (i + 1) * LANES] = term
            rest = rest - term.astype(jnp.float32)

    later = total - earlier - lane_total

    @pl.when(first_core)
    def _():
        pack(off_chip_ref, earlier, range(tiles))
        pack(on_chip_ref, later, range(tiles - 1, -1, -1))

    @pl.when(jnp.logical_not(first_core))
    def _():
        pack(on_chip_ref, earlier, range(tiles))
        pack(off_chip_ref, later, range(tiles - 1, -1, -1))


def normalize_kernel(place_ref, filtered_ref, total_ref, on_chip_ref, off_chip_ref, out_ref):
    channels, length = filtered_ref.shape
    tiles = length // LANES
    count = place_ref[3]
    base = total_ref[...]
    for i in range(3):
        cols = slice(length + i * LANES, length + (i + 1) * LANES)
        base = base + on_chip_ref[:, cols].astype(jnp.float32)
        base = base + off_chip_ref[:, cols].astype(jnp.float32)
    lane = lax.broadcasted_iota(jnp.int32, (channels, LANES), 1)
    for r in range(tiles):
        cols = slice(r * LANES, (r + 1) * LANES)
        time = place_ref[2] * length + tiles * lane + r
        upper = jnp.minimum(time + length, length * count - 1) + 1
        lower = jnp.maximum(time - length, 0)
        window = base + (
            on_chip_ref[:, cols].astype(jnp.float32) + off_chip_ref[:, cols].astype(jnp.float32)
        )
        level = window / (upper - lower).astype(jnp.float32)
        out_ref[:, cols] = (filtered_ref[:, cols] / (level + 1e-06)).astype(jnp.bfloat16)


def normalize(raw, band_index, filter_taps, place):
    channels, length = raw.shape
    first_core = place[1] == 0
    low, high = raw[:, :HF].T, raw[:, length - HF :].T
    inner, outer = to_neighbours(
        jnp.where(first_core, high, low), jnp.where(first_core, low, high)
    )
    band = band_index[None, :]
    coeff = jnp.broadcast_to(filter_taps[NBANDS - 1][:, None], (TAPS, channels))
    for i in range(NBANDS - 1):
        coeff = jnp.where(band == i, filter_taps[i][:, None], coeff)
    vmem = pl.BlockSpec(memory_space=pltpu.VMEM)
    smem = pl.BlockSpec(memory_space=pltpu.SMEM)
    packed = jax.ShapeDtypeStruct((channels, length + 3 * LANES), jnp.bfloat16)
    filtered, total, on_chip, off_chip = pl.pallas_call(
        filter_kernel,
        out_shape=(
            jax.ShapeDtypeStruct((channels, length), jnp.float32),
            jax.ShapeDtypeStruct((channels, LANES), jnp.float32),
            packed,
            packed,
        ),
        in_specs=[smem] + [vmem] * 4,
        out_specs=(vmem,) * 4,
        scratch_shapes=[
            pltpu.VMEM((length + 2 * HF, channels), jnp.float32),
            pltpu.VMEM((length, channels), jnp.float32),
        ],
        compiler_params=pltpu.CompilerParams(vmem_limit_bytes=24 * 1024 * 1024),
        name="filter",
    )(place, coeff, raw.T, inner, outer)
    on_chip, off_chip = to_neighbours(on_chip, off_chip)
    return pl.pallas_call(
        normalize_kernel,
        out_shape=jax.ShapeDtypeStruct((channels, length), jnp.bfloat16),
        in_specs=[smem] + [vmem] * 4,
        out_specs=vmem,
        compiler_params=pltpu.CompilerParams(vmem_limit_bytes=24 * 1024 * 1024),
        name="normalize",
    )(place, filtered, total, on_chip, off_chip)


def lagged_kernel(
    count, scale, place_ref, row_hbm, part_hbm, out_hbm, fan, both, carry, acc, row_buf, part_buf, out_buf, row_sem, part_sem, out_sem
):
    rows = row_buf.shape[1]
    channels, length = part_buf.shape[1:]
    tiles = length // LANES
    reach = -(-LAGH // tiles)
    lead = reach * tiles + LAGH
    first_row = pl.multiple_of(place_ref[1] * rows, rows)

    def row_copy(t):
        return pltpu.make_async_copy(
            row_hbm.at[place_ref[0] + t, pl.ds(first_row, rows)], row_buf.at[t + 1], row_sem.at[t]
        )

    def part_copy(t):
        return pltpu.make_async_copy(
            part_hbm.at[place_ref[2] + t], part_buf.at[t], part_sem.at[t]
        )

    for t in range(AHEAD):
        row_copy(t).start()
        part_copy(t).start()
    acc[...] = jnp.zeros_like(acc)
    carry[...] = jnp.zeros_like(carry)
    row_buf[0] = jnp.zeros((rows, length), jnp.bfloat16)
    row_buf[count + 1] = jnp.zeros((rows, length), jnp.bfloat16)
    lane = lax.broadcasted_iota(jnp.int32, (rows, length), 1) % LANES
    part_lane = lax.broadcasted_iota(jnp.int32, (channels, LANES), 1)
    row_copy(0).wait()

    def moved(width, offset):
        return jnp.concatenate(
            [
                fan[:, (lead - 2 * a + offset) * LANES : (lead - 2 * a + offset + width) * LANES]
                for a in range(PAIRS)
            ],
            axis=0,
        )

    def body(step, unused):
        @pl.when(step + AHEAD < count)
        def _():
            row_copy(step + AHEAD).start()
            part_copy(step + AHEAD).start()

        @pl.when(step + 1 < count)
        def _():
            row_copy(step + 1).wait()

        inside = row_buf[step + 1].astype(jnp.float32)
        left = row_buf[step].astype(jnp.float32)
        right = row_buf[step + 2].astype(jnp.float32)
        for j in range(-reach, reach + 1):
            if j < 0:
                mixed = jnp.where(lane >= LANES + j, left, inside)
            else:
                mixed = jnp.where(lane < j, right, inside)
            for r in range(tiles):
                tile = mixed[:, r * LANES : (r + 1) * LANES]
                if j != 0:
                    tile = pltpu.roll(tile, (-j) % LANES, 1)
                at = (j + reach) * tiles + r
                fan[:, at * LANES : (at + 1) * LANES] = tile.astype(jnp.bfloat16)

        part_copy(step).wait()
        both[:channels] = part_buf[step]
        both[channels:, LANES:] = part_buf[step, :, : length - LANES]
        final = part_buf[step, :, length - LANES :].astype(jnp.float32)
        late = pltpu.roll(jnp.where(part_lane == LANES - 1, carry[...], final), 1, 1)
        both[channels:, :LANES] = late.astype(jnp.bfloat16)
        carry[...] = final
        acc[...] += lax.dot_general(
            moved(tiles, 0), both[...], (((1,), (1,)), ((), ())), preferred_element_type=jnp.float32
        )
        return unused

    lax.fori_loop(0, count, body, 0)
    tail = jnp.where(part_lane == LANES - 1, carry[...], 0.0).astype(jnp.bfloat16)
    acc[:, channels:] += lax.dot_general(
        moved(1, tiles), tail, (((1,), (1,)), ((), ())), preferred_element_type=jnp.float32
    )
    outs = []
    for a in range(PAIRS):
        block = acc[a * rows : (a + 1) * rows] * scale
        out_buf[2 * a] = block[:, :channels].astype(out_buf.dtype)
        if a > 0:
            out_buf[2 * a - 1] = block[:, channels:].astype(out_buf.dtype)
        if a in (PAIRS // 2, PAIRS - 1):
            done = 2 * (PAIRS // 2) + 1 if outs else 0
            span = pl.ds(done, 2 * a + 1 - done)
            outs.append(
                pltpu.make_async_copy(
                    out_buf.at[span], out_hbm.at[out_hbm.shape[0] - 1, span], out_sem.at[len(outs)]
                )
            )
            outs[-1].start()
    for copy in outs:
        copy.wait()


def lagged(place, own_rows, partner, rows, count, scale, out_dtype, rounds):
    channels, length = partner.shape[1:]
    tiles = length // LANES
    fan_tiles = (2 * -(-LAGH // tiles) + 1) * tiles
    anywhere = pl.BlockSpec(memory_space=pl.ANY)
    return pl.pallas_call(
        functools.partial(lagged_kernel, count, scale),
        out_shape=jax.ShapeDtypeStruct((rounds, LAGS, rows, channels), out_dtype),
        in_specs=[pl.BlockSpec(memory_space=pltpu.SMEM), anywhere, anywhere],
        out_specs=anywhere,
        scratch_shapes=[
            pltpu.VMEM((rows, fan_tiles * LANES), jnp.bfloat16),
            pltpu.VMEM((2 * channels, length), jnp.bfloat16),
            pltpu.VMEM((channels, LANES), jnp.float32),
            pltpu.VMEM((PAIRS * rows, 2 * channels), jnp.float32),
            pltpu.VMEM((count + 2, rows, length), jnp.bfloat16),
            pltpu.VMEM((count, channels, length), jnp.bfloat16),
            pltpu.VMEM((LAGS, rows, channels), out_dtype),
            pltpu.SemaphoreType.DMA((count,)),
            pltpu.SemaphoreType.DMA((count,)),
            pltpu.SemaphoreType.DMA((2,)),
        ],
        compiler_params=pltpu.CompilerParams(vmem_limit_bytes=VMEM_BYTES),
        cost_estimate=pl.CostEstimate(
            flops=4 * count * PAIRS * rows * channels * length,
            bytes_accessed=2 * count * channels * length,
            transcendentals=0,
        ),
        name="lagged",
    )(place, own_rows, partner)


def on_device(raw_strain, band_index, filter_taps):
    channels, length = raw_strain.shape
    count = lax.axis_size("ta")
    rows = channels // count
    scale = 1.0 / math.sqrt(length * count)
    swap = [(0, 1), (1, 0)]
    half, upper, piece = lax.axis_index("zh"), lax.axis_index("cp"), lax.axis_index("ta")

    zero = 0 * piece
    here = jnp.stack([zero, piece % 2, piece, zero + count]).astype(jnp.int32)
    normalized = normalize(raw_strain, band_index, filter_taps, here)
    ring = lax.all_gather(normalized, ("zh", "ta"), axis=0, tiled=False)
    guest = lax.all_to_all(normalized.reshape(count, rows, length), "ta", 0, 0)
    guest = lax.ppermute(guest, "cp", swap)

    other = (1 - half) * count
    near = jnp.where(upper == 1, other, half * count)
    place0 = jnp.stack([zero, zero, near]).astype(jnp.int32)
    place1 = jnp.stack([half * count, piece, other]).astype(jnp.int32)
    first = lagged(place0, guest, ring, rows, count, scale, jnp.bfloat16, 1)
    place1, first = lax.optimization_barrier((place1, first))
    first = lax.ppermute(first, "cp", swap)
    result = lagged(place1, ring, ring, rows, count, scale, jnp.float32, ROUNDS)
    return lax.dynamic_update_slice_in_dim(result, first.astype(jnp.float32), 0, 0)


def solution(mesh):
    blocks, slices = mesh.devices.shape
    axes = ("zh", "cp", "col", "ta")
    parts = Mesh(mesh.devices.reshape(2, 2, blocks // 4, slices), axes)
    channel_axes = axes[:3]
    return jax.shard_map(
        on_device,
        mesh=parts,
        in_specs=(P(channel_axes, "ta"), P(channel_axes), P()),
        out_specs=P(None, None, axes, None),
        check_vma=False,
    )
```

```python
import functools
import math

import jax
import jax.numpy as jnp
from jax import lax
from jax.experimental import pallas as pl
from jax.experimental.pallas import tpu as pltpu
from jax.sharding import Mesh
from jax.sharding import PartitionSpec as P

HF = 16
TAPS = 33
NBANDS = 4
LAGH = 32
LAGS = 65
PAIRS = LAGH + 1
LANES = 128
AHEAD = 3
ROUNDS = 2
CHUNK = 64
VMEM_BYTES = 52 * 1024 * 1024


def to_neighbours(on_chip, off_chip):
    count = lax.axis_size("ta")
    inner = [(i, i ^ 1) for i in range(count)]
    outer = [(i, i - 1 + 2 * (i % 2)) for i in range(1, count - 1)]
    off_chip = lax.ppermute(off_chip, "ta", outer)
    return lax.ppermute(on_chip, "ta", inner), off_chip


def filter_kernel(
    place_ref, coeff_ref, tall_ref, inner_ref, outer_ref, out_ref, total_ref, lanes_ref, off_chip_ref, tall, wide
):
    length, channels = tall_ref.shape
    tiles = length // LANES
    first_core = place_ref[1] == 0
    tall[:HF] = jnp.where(first_core, outer_ref[...], inner_ref[...]).T[LANES - HF :]
    tall[HF : HF + length] = tall_ref[...]
    tall[HF + length :] = jnp.where(first_core, inner_ref[...], outer_ref[...]).T[:HF]

    def chunk(i, carry):
        base = pl.multiple_of(i * CHUNK, CHUNK)
        total = jnp.zeros((CHUNK, channels), jnp.float32)
        for k in range(TAPS):
            total = total + coeff_ref[k : k + 1, :] * tall[pl.ds(base + k, CHUNK), :]
        wide[pl.ds(base, CHUNK), :] = total
        return carry

    lax.fori_loop(0, length // CHUNK, chunk, 0)
    lane_total = jnp.zeros((channels, LANES), jnp.float32)
    for r in range(tiles):
        piece = wide[pl.ds(r, LANES, stride=tiles), :].T
        out_ref[:, r * LANES : (r + 1) * LANES] = piece
        lane_total = lane_total + jnp.abs(piece)
    row = lax.broadcasted_iota(jnp.int32, (LANES, LANES), 0)
    col = lax.broadcasted_iota(jnp.int32, (LANES, LANES), 1)
    earlier = jnp.dot(
        lane_total,
        (row < col).astype(jnp.float32),
        precision=lax.Precision.HIGHEST,
        preferred_element_type=jnp.float32,
    )
    total = jnp.broadcast_to((earlier + lane_total)[:, LANES - 1 :], (channels, LANES))
    total_ref[...] = total

    later = total - earlier - lane_total
    lanes_ref[...] = jnp.where(first_core, later, earlier)

    @pl.when(first_core)
    def _():
        pack(off_chip_ref, out_ref, earlier, range(tiles))

    @pl.when(jnp.logical_not(first_core))
    def _():
        pack(off_chip_ref, out_ref, later, range(tiles - 1, -1, -1))


def pack(ref, filtered_ref, lanes_sum, order):
    channels, length = filtered_ref.shape
    inner = jnp.zeros((channels, LANES), jnp.float32)
    for r in order:
        cols = slice(r * LANES, (r + 1) * LANES)
        inner = inner + jnp.abs(filtered_ref[:, cols])
        ref[:, cols] = inner.astype(jnp.bfloat16)
    rest = lanes_sum
    for i in range(ref.shape[1] // LANES - len(order)):
        term = rest.astype(jnp.bfloat16)
        ref[:, length + i * LANES : length + (i + 1) * LANES] = term
        rest = rest - term.astype(jnp.float32)


def pack_kernel(place_ref, filtered_ref, lanes_ref, on_chip_ref):
    tiles = filtered_ref.shape[1] // LANES
    first_core = place_ref[1] == 0

    @pl.when(first_core)
    def _():
        pack(on_chip_ref, filtered_ref, lanes_ref[...], range(tiles - 1, -1, -1))

    @pl.when(jnp.logical_not(first_core))
    def _():
        pack(on_chip_ref, filtered_ref, lanes_ref[...], range(tiles))


def normalize_kernel(place_ref, filtered_ref, total_ref, on_chip_ref, off_chip_ref, out_ref):
    channels, length = filtered_ref.shape
    tiles = length // LANES
    count = place_ref[3]
    base = total_ref[...]
    for ref in (on_chip_ref, off_chip_ref):
        for start in range(length, ref.shape[1], LANES):
            base = base + ref[:, start : start + LANES].astype(jnp.float32)
    lane = lax.broadcasted_iota(jnp.int32, (channels, LANES), 1)
    for r in range(tiles):
        cols = slice(r * LANES, (r + 1) * LANES)
        time = place_ref[2] * length + tiles * lane + r
        upper = jnp.minimum(time + length, length * count - 1) + 1
        lower = jnp.maximum(time - length, 0)
        window = base + (
            on_chip_ref[:, cols].astype(jnp.float32) + off_chip_ref[:, cols].astype(jnp.float32)
        )
        level = window / (upper - lower).astype(jnp.float32)
        out_ref[:, cols] = (filtered_ref[:, cols] / (level + 1e-06)).astype(jnp.bfloat16)


def normalize(raw, band_index, filter_taps, place):
    channels, length = raw.shape
    first_core = place[1] == 0
    low, high = raw[:, :LANES], raw[:, length - LANES :]
    inner, outer = to_neighbours(
        jnp.where(first_core, high, low), jnp.where(first_core, low, high)
    )
    band = band_index[None, :]
    coeff = jnp.broadcast_to(filter_taps[NBANDS - 1][:, None], (TAPS, channels))
    for i in range(NBANDS - 1):
        coeff = jnp.where(band == i, filter_taps[i][:, None], coeff)
    vmem = pl.BlockSpec(memory_space=pltpu.VMEM)
    smem = pl.BlockSpec(memory_space=pltpu.SMEM)
    packed = jax.ShapeDtypeStruct((channels, length + 3 * LANES), jnp.bfloat16)
    lanes = jax.ShapeDtypeStruct((channels, LANES), jnp.float32)
    filtered, total, part, off_chip = pl.pallas_call(
        filter_kernel,
        out_shape=(
            jax.ShapeDtypeStruct((channels, length), jnp.float32),
            lanes,
            lanes,
            packed,
        ),
        in_specs=[smem] + [vmem] * 4,
        out_specs=(vmem,) * 4,
        scratch_shapes=[
            pltpu.VMEM((length + 2 * HF, channels), jnp.float32),
            pltpu.VMEM((length, channels), jnp.float32),
        ],
        compiler_params=pltpu.CompilerParams(vmem_limit_bytes=24 * 1024 * 1024),
        name="filter",
    )(place, coeff, lax.optimization_barrier(raw).T, inner, outer)
    on_chip = pl.pallas_call(
        pack_kernel,
        out_shape=jax.ShapeDtypeStruct((channels, length + 2 * LANES), jnp.bfloat16),
        in_specs=[smem, vmem, vmem],
        out_specs=vmem,
        compiler_params=pltpu.CompilerParams(vmem_limit_bytes=24 * 1024 * 1024),
        cost_estimate=pl.CostEstimate(
            flops=2 * channels * length, bytes_accessed=16 * channels * length, transcendentals=0
        ),
        name="pack",
    )(place, filtered, part)
    on_chip, off_chip = to_neighbours(on_chip, off_chip)
    return pl.pallas_call(
        normalize_kernel,
        out_shape=jax.ShapeDtypeStruct((channels, length), jnp.bfloat16),
        in_specs=[smem] + [vmem] * 4,
        out_specs=vmem,
        compiler_params=pltpu.CompilerParams(vmem_limit_bytes=24 * 1024 * 1024),
        name="normalize",
    )(place, filtered, total, on_chip, off_chip)


def lagged_kernel(
    count, scale, place_ref, row_hbm, part_hbm, out_hbm, fan, both, carry, acc, row_buf, part_buf, row_sem, part_sem, *buffer
):
    out_buf, out_sem = buffer if buffer else (out_hbm.at[0], None)
    rows = row_buf.shape[1]
    channels, length = part_buf.shape[1:]
    tiles = length // LANES
    reach = -(-LAGH // tiles)
    lead = reach * tiles + LAGH
    first_row = pl.multiple_of(place_ref[1] * rows, rows)

    def row_copy(t):
        return pltpu.make_async_copy(
            row_hbm.at[place_ref[0] + t, pl.ds(first_row, rows)], row_buf.at[t + 1], row_sem.at[t]
        )

    def part_copy(t):
        return pltpu.make_async_copy(
            part_hbm.at[place_ref[2] + t], part_buf.at[t], part_sem.at[t]
        )

    for t in range(AHEAD):
        row_copy(t).start()
        part_copy(t).start()
    acc[...] = jnp.zeros_like(acc)
    carry[...] = jnp.zeros_like(carry)
    row_buf[0] = jnp.zeros((rows, length), jnp.bfloat16)
    row_buf[count + 1] = jnp.zeros((rows, length), jnp.bfloat16)
    lane = lax.broadcasted_iota(jnp.int32, (rows, length), 1) % LANES
    part_lane = lax.broadcasted_iota(jnp.int32, (channels, LANES), 1)
    row_copy(0).wait()

    def moved(width, offset):
        return jnp.concatenate(
            [
                fan[:, (lead - 2 * a + offset) * LANES : (lead - 2 * a + offset + width) * LANES]
                for a in range(PAIRS)
            ],
            axis=0,
        )

    def body(step, unused):
        @pl.when(step + AHEAD < count)
        def _():
            row_copy(step + AHEAD).start()
            part_copy(step + AHEAD).start()

        @pl.when(step + 1 < count)
        def _():
            row_copy(step + 1).wait()

        inside = row_buf[step + 1].astype(jnp.float32)
        left = row_buf[step].astype(jnp.float32)
        right = row_buf[step + 2].astype(jnp.float32)
        for j in range(-reach, reach + 1):
            if j < 0:
                mixed = jnp.where(lane >= LANES + j, left, inside)
            else:
                mixed = jnp.where(lane < j, right, inside)
            for r in range(tiles):
                tile = mixed[:, r * LANES : (r + 1) * LANES]
                if j != 0:
                    tile = pltpu.roll(tile, (-j) % LANES, 1)
                at = (j + reach) * tiles + r
                fan[:, at * LANES : (at + 1) * LANES] = tile.astype(jnp.bfloat16)

        part_copy(step).wait()
        both[:channels] = part_buf[step]
        both[channels:, LANES:] = part_buf[step, :, : length - LANES]
        final = part_buf[step, :, length - LANES :].astype(jnp.float32)
        late = pltpu.roll(jnp.where(part_lane == LANES - 1, carry[...], final), 1, 1)
        both[channels:, :LANES] = late.astype(jnp.bfloat16)
        carry[...] = final
        acc[...] += lax.dot_general(
            moved(tiles, 0), both[...], (((1,), (1,)), ((), ())), preferred_element_type=jnp.float32
        )
        return unused

    lax.fori_loop(0, count, body, 0)
    tail = jnp.where(part_lane == LANES - 1, carry[...], 0.0).astype(jnp.bfloat16)
    acc[:, channels:] += lax.dot_general(
        moved(1, tiles), tail, (((1,), (1,)), ((), ())), preferred_element_type=jnp.float32
    )
    outs = []
    for a in range(PAIRS):
        block = acc[a * rows : (a + 1) * rows] * scale
        out_buf[2 * a] = block[:, :channels].astype(out_buf.dtype)
        if a > 0:
            out_buf[2 * a - 1] = block[:, channels:].astype(out_buf.dtype)
        if buffer and a in (PAIRS // 2, PAIRS - 1):
            done = 2 * (PAIRS // 2) + 1 if outs else 0
            span = pl.ds(done, 2 * a + 1 - done)
            outs.append(
                pltpu.make_async_copy(
                    out_buf.at[span], out_hbm.at[out_hbm.shape[0] - 1, span], out_sem.at[len(outs)]
                )
            )
            outs[-1].start()
    for copy in outs:
        copy.wait()


def lagged(place, own_rows, partner, rows, count, scale, out_dtype, rounds):
    channels, length = partner.shape[1:]
    tiles = length // LANES
    fan_tiles = (2 * -(-LAGH // tiles) + 1) * tiles
    anywhere = pl.BlockSpec(memory_space=pl.ANY)
    buffer = []
    if rounds > 1:
        buffer = [pltpu.VMEM((LAGS, rows, channels), out_dtype), pltpu.SemaphoreType.DMA((2,))]
    return pl.pallas_call(
        functools.partial(lagged_kernel, count, scale),
        out_shape=jax.ShapeDtypeStruct((rounds, LAGS, rows, channels), out_dtype),
        in_specs=[pl.BlockSpec(memory_space=pltpu.SMEM), anywhere, anywhere],
        out_specs=anywhere if buffer else pl.BlockSpec(memory_space=pltpu.VMEM),
        scratch_shapes=[
            pltpu.VMEM((rows, fan_tiles * LANES), jnp.bfloat16),
            pltpu.VMEM((2 * channels, length), jnp.bfloat16),
            pltpu.VMEM((channels, LANES), jnp.float32),
            pltpu.VMEM((PAIRS * rows, 2 * channels), jnp.float32),
            pltpu.VMEM((count + 2, rows, length), jnp.bfloat16),
            pltpu.VMEM((count, channels, length), jnp.bfloat16),
            pltpu.SemaphoreType.DMA((count,)),
            pltpu.SemaphoreType.DMA((count,)),
        ]
        + buffer,
        compiler_params=pltpu.CompilerParams(vmem_limit_bytes=VMEM_BYTES),
        cost_estimate=pl.CostEstimate(
            flops=4 * count * PAIRS * rows * channels * length,
            bytes_accessed=2 * count * channels * length,
            transcendentals=0,
        ),
        name="lagged",
    )(place, own_rows, partner)


def on_device(raw_strain, band_index, filter_taps):
    channels, length = raw_strain.shape
    count = lax.axis_size("ta")
    rows = channels // count
    scale = 1.0 / math.sqrt(length * count)
    swap = [(0, 1), (1, 0)]
    half, upper, piece = lax.axis_index("zh"), lax.axis_index("cp"), lax.axis_index("ta")

    zero = 0 * piece
    here = jnp.stack([zero, piece % 2, piece, zero + count]).astype(jnp.int32)
    normalized = normalize(raw_strain, band_index, filter_taps, here)
    ring = lax.all_gather(normalized, ("zh", "ta"), axis=0, tiled=False)
    guest = lax.all_to_all(normalized.reshape(count, rows, length), "ta", 0, 0)
    guest = lax.ppermute(guest, "cp", swap)

    other = (1 - half) * count
    near = jnp.where(upper == 1, other, half * count)
    place0 = jnp.stack([zero, zero, near]).astype(jnp.int32)
    place1 = jnp.stack([half * count, piece, other]).astype(jnp.int32)
    first = lagged(place0, guest, ring, rows, count, scale, jnp.bfloat16, 1)
    place1, first = lax.optimization_barrier((place1, first))
    first = lax.ppermute(first, "cp", swap)
    result = lagged(place1, ring, ring, rows, count, scale, jnp.float32, ROUNDS)
    return lax.dynamic_update_slice_in_dim(result, first.astype(jnp.float32), 0, 0)


def solution(mesh):
    blocks, slices = mesh.devices.shape
    axes = ("zh", "cp", "col", "ta")
    parts = Mesh(mesh.devices.reshape(2, 2, blocks // 4, slices), axes)
    channel_axes = axes[:3]
    return jax.shard_map(
        on_device,
        mesh=parts,
        in_specs=(P(channel_axes, "ta"), P(channel_axes), P()),
        out_specs=P(None, None, axes, None),
        check_vma=False,
    )
```

```python
import functools
import math

import jax
import jax.numpy as jnp
from jax import lax
from jax.experimental import pallas as pl
from jax.experimental.pallas import tpu as pltpu
from jax.sharding import Mesh
from jax.sharding import PartitionSpec as P

HF = 16
TAPS = 33
NBANDS = 4
LAGH = 32
LAGS = 65
PAIRS = LAGH + 1
LANES = 128
AHEAD = 3
ROUNDS = 2
CHUNK = 64
VMEM_BYTES = 52 * 1024 * 1024


def to_neighbours(on_chip, off_chip):
    count = lax.axis_size("ta")
    inner = [(i, i ^ 1) for i in range(count)]
    outer = [(i, i - 1 + 2 * (i % 2)) for i in range(1, count - 1)]
    off_chip = lax.ppermute(off_chip, "ta", outer)
    return lax.ppermute(on_chip, "ta", inner), off_chip


def filter_kernel(
    place_ref, coeff_ref, tall_ref, inner_ref, outer_ref, out_ref, total_ref, lanes_ref, off_chip_ref, tall, wide
):
    length, channels = tall_ref.shape
    tiles = length // LANES
    first_core = place_ref[1] == 0
    tall[:HF] = jnp.where(first_core, outer_ref[...], inner_ref[...]).T[LANES - HF :]
    tall[HF : HF + length] = tall_ref[...]
    tall[HF + length :] = jnp.where(first_core, inner_ref[...], outer_ref[...]).T[:HF]

    def chunk(i, carry):
        base = pl.multiple_of(i * CHUNK, CHUNK)
        total = jnp.zeros((CHUNK, channels), jnp.float32)
        for k in range(TAPS):
            total = total + coeff_ref[k : k + 1, :] * tall[pl.ds(base + k, CHUNK), :]
        wide[pl.ds(base, CHUNK), :] = total
        return carry

    lax.fori_loop(0, length // CHUNK, chunk, 0)
    lane_total = jnp.zeros((channels, LANES), jnp.float32)
    for r in range(tiles):
        piece = wide[pl.ds(r, LANES, stride=tiles), :].T
        out_ref[:, r * LANES : (r + 1) * LANES] = piece
        lane_total = lane_total + jnp.abs(piece)
    row = lax.broadcasted_iota(jnp.int32, (LANES, LANES), 0)
    col = lax.broadcasted_iota(jnp.int32, (LANES, LANES), 1)
    earlier = jnp.dot(
        lane_total,
        (row < col).astype(jnp.float32),
        precision=lax.Precision.HIGHEST,
        preferred_element_type=jnp.float32,
    )
    total = jnp.broadcast_to((earlier + lane_total)[:, LANES - 1 :], (channels, LANES))
    total_ref[...] = total

    later = total - earlier - lane_total
    lanes_ref[...] = jnp.where(first_core, later, earlier)

    @pl.when(first_core)
    def _():
        pack(off_chip_ref, out_ref, earlier, range(tiles))

    @pl.when(jnp.logical_not(first_core))
    def _():
        pack(off_chip_ref, out_ref, later, range(tiles - 1, -1, -1))


def pack(ref, filtered_ref, lanes_sum, order):
    channels, length = filtered_ref.shape
    inner = jnp.zeros((channels, LANES), jnp.float32)
    for r in order:
        cols = slice(r * LANES, (r + 1) * LANES)
        inner = inner + jnp.abs(filtered_ref[:, cols])
        ref[:, cols] = inner.astype(jnp.bfloat16)
    rest = lanes_sum
    for i in range(ref.shape[1] // LANES - len(order)):
        term = rest.astype(jnp.bfloat16)
        ref[:, length + i * LANES : length + (i + 1) * LANES] = term
        rest = rest - term.astype(jnp.float32)


def pack_kernel(place_ref, filtered_ref, lanes_ref, on_chip_ref):
    tiles = filtered_ref.shape[1] // LANES
    first_core = place_ref[1] == 0

    @pl.when(first_core)
    def _():
        pack(on_chip_ref, filtered_ref, lanes_ref[...], range(tiles - 1, -1, -1))

    @pl.when(jnp.logical_not(first_core))
    def _():
        pack(on_chip_ref, filtered_ref, lanes_ref[...], range(tiles))


def normalize_kernel(place_ref, filtered_ref, total_ref, on_chip_ref, off_chip_ref, out_ref):
    channels, length = filtered_ref.shape
    tiles = length // LANES
    count = place_ref[3]
    base = total_ref[...]
    for ref in (on_chip_ref, off_chip_ref):
        for start in range(length, ref.shape[1], LANES):
            base = base + ref[:, start : start + LANES].astype(jnp.float32)
    lane = lax.broadcasted_iota(jnp.int32, (channels, LANES), 1)
    for r in range(tiles):
        cols = slice(r * LANES, (r + 1) * LANES)
        time = place_ref[2] * length + tiles * lane + r
        upper = jnp.minimum(time + length, length * count - 1) + 1
        lower = jnp.maximum(time - length, 0)
        window = base + (
            on_chip_ref[:, cols].astype(jnp.float32) + off_chip_ref[:, cols].astype(jnp.float32)
        )
        level = window / (upper - lower).astype(jnp.float32)
        out_ref[:, cols] = (filtered_ref[:, cols] / (level + 1e-06)).astype(jnp.bfloat16)


def normalize(raw, band_index, filter_taps, place):
    channels, length = raw.shape
    first_core = place[1] == 0
    low, high = raw[:, :LANES], raw[:, length - LANES :]
    inner, outer = to_neighbours(
        jnp.where(first_core, high, low), jnp.where(first_core, low, high)
    )
    chosen = (jnp.arange(NBANDS, dtype=jnp.int32)[:, None] == band_index[None, :]).astype(jnp.float32)
    coeff = lax.dot_general(
        filter_taps,
        chosen,
        (((0,), (0,)), ((), ())),
        precision=lax.Precision.HIGHEST,
        preferred_element_type=jnp.float32,
    )
    vmem = pl.BlockSpec(memory_space=pltpu.VMEM)
    smem = pl.BlockSpec(memory_space=pltpu.SMEM)
    packed = jax.ShapeDtypeStruct((channels, length + 3 * LANES), jnp.bfloat16)
    lanes = jax.ShapeDtypeStruct((channels, LANES), jnp.float32)
    filtered, total, part, off_chip = pl.pallas_call(
        filter_kernel,
        out_shape=(
            jax.ShapeDtypeStruct((channels, length), jnp.float32),
            lanes,
            lanes,
            packed,
        ),
        in_specs=[smem] + [vmem] * 4,
        out_specs=(vmem,) * 4,
        scratch_shapes=[
            pltpu.VMEM((length + 2 * HF, channels), jnp.float32),
            pltpu.VMEM((length, channels), jnp.float32),
        ],
        compiler_params=pltpu.CompilerParams(vmem_limit_bytes=24 * 1024 * 1024),
        name="filter",
    )(place, coeff, lax.optimization_barrier(raw).T, inner, outer)
    on_chip = pl.pallas_call(
        pack_kernel,
        out_shape=jax.ShapeDtypeStruct((channels, length + 2 * LANES), jnp.bfloat16),
        in_specs=[smem, vmem, vmem],
        out_specs=vmem,
        compiler_params=pltpu.CompilerParams(vmem_limit_bytes=24 * 1024 * 1024),
        cost_estimate=pl.CostEstimate(
            flops=2 * channels * length, bytes_accessed=16 * channels * length, transcendentals=0
        ),
        name="pack",
    )(place, filtered, part)
    on_chip, off_chip = to_neighbours(on_chip, off_chip)
    return pl.pallas_call(
        normalize_kernel,
        out_shape=jax.ShapeDtypeStruct((channels, length), jnp.bfloat16),
        in_specs=[smem] + [vmem] * 4,
        out_specs=vmem,
        compiler_params=pltpu.CompilerParams(vmem_limit_bytes=24 * 1024 * 1024),
        name="normalize",
    )(place, filtered, total, on_chip, off_chip)


def fan_kernel(row_ref, out_ref):
    count, rows, length = row_ref.shape
    tiles = length // LANES
    reach = -(-LAGH // tiles)
    lane = lax.broadcasted_iota(jnp.int32, (rows, length), 1) % LANES

    def body(step, unused):
        inside = row_ref[step].astype(jnp.float32)
        left = row_ref[jnp.maximum(step - 1, 0)].astype(jnp.float32)
        left = jnp.where(step > 0, left, 0.0)
        right = row_ref[jnp.minimum(step + 1, count - 1)].astype(jnp.float32)
        right = jnp.where(step < count - 1, right, 0.0)
        for j in range(-reach, reach + 1):
            if j < 0:
                mixed = jnp.where(lane >= LANES + j, left, inside)
            else:
                mixed = jnp.where(lane < j, right, inside)
            for r in range(tiles):
                tile = mixed[:, r * LANES : (r + 1) * LANES]
                if j != 0:
                    tile = pltpu.roll(tile, (-j) % LANES, 1)
                at = (j + reach) * tiles + r
                out_ref[step, :, at * LANES : (at + 1) * LANES] = tile.astype(jnp.bfloat16)
        return unused

    lax.fori_loop(0, count, body, 0)


def fan_of(own_rows):
    count, rows, length = own_rows.shape
    tiles = length // LANES
    fan_tiles = (2 * -(-LAGH // tiles) + 1) * tiles
    vmem = pl.BlockSpec(memory_space=pltpu.VMEM)
    return pl.pallas_call(
        fan_kernel,
        out_shape=jax.ShapeDtypeStruct((count, rows, fan_tiles * LANES), jnp.bfloat16),
        in_specs=[vmem],
        out_specs=vmem,
        compiler_params=pltpu.CompilerParams(vmem_limit_bytes=24 * 1024 * 1024),
        cost_estimate=pl.CostEstimate(
            flops=20 * count * rows * fan_tiles * LANES,
            bytes_accessed=2 * count * rows * fan_tiles * LANES,
            transcendentals=0,
        ),
        name="fan",
    )(own_rows)


def lagged_kernel(
    count, scale, place_ref, fan_hbm, part_hbm, out_hbm, fan_buf, both, carry, acc, part_buf, fan_sem, part_sem, *buffer
):
    out_buf, out_sem = buffer if buffer else (out_hbm.at[0], None)
    rows = fan_buf.shape[1]
    channels, length = part_buf.shape[1:]
    tiles = length // LANES
    lead = -(-LAGH // tiles) * tiles + LAGH

    def part_copy(t):
        return pltpu.make_async_copy(
            part_hbm.at[place_ref[0] + t], part_buf.at[t], part_sem.at[t]
        )

    def fan_copy(t):
        return pltpu.make_async_copy(fan_hbm.at[t], fan_buf.at[t], fan_sem.at[t])

    for t in range(AHEAD):
        part_copy(t).start()
        fan_copy(t).start()
    acc[...] = jnp.zeros_like(acc)
    carry[...] = jnp.zeros_like(carry)
    part_lane = lax.broadcasted_iota(jnp.int32, (channels, LANES), 1)

    def moved(step, width, offset):
        return jnp.concatenate(
            [
                fan_buf[
                    step, :, (lead - 2 * a + offset) * LANES : (lead - 2 * a + offset + width) * LANES
                ]
                for a in range(PAIRS)
            ],
            axis=0,
        )

    def body(step, unused):
        @pl.when(step + AHEAD < count)
        def _():
            part_copy(step + AHEAD).start()
            fan_copy(step + AHEAD).start()

        part_copy(step).wait()
        both[:channels] = part_buf[step]
        both[channels:, LANES:] = part_buf[step, :, : length - LANES]
        final = part_buf[step, :, length - LANES :].astype(jnp.float32)
        late = pltpu.roll(jnp.where(part_lane == LANES - 1, carry[...], final), 1, 1)
        both[channels:, :LANES] = late.astype(jnp.bfloat16)
        carry[...] = final
        fan_copy(step).wait()
        acc[...] += lax.dot_general(
            moved(step, tiles, 0),
            both[...],
            (((1,), (1,)), ((), ())),
            preferred_element_type=jnp.float32,
        )
        return unused

    lax.fori_loop(0, count, body, 0)
    tail = jnp.where(part_lane == LANES - 1, carry[...], 0.0).astype(jnp.bfloat16)
    acc[:, channels:] += lax.dot_general(
        moved(count - 1, 1, tiles),
        tail,
        (((1,), (1,)), ((), ())),
        preferred_element_type=jnp.float32,
    )
    outs = []
    for a in range(PAIRS):
        block = acc[a * rows : (a + 1) * rows] * scale
        out_buf[2 * a] = block[:, :channels].astype(out_buf.dtype)
        if a > 0:
            out_buf[2 * a - 1] = block[:, channels:].astype(out_buf.dtype)
        if buffer and a in (PAIRS // 2, PAIRS - 1):
            done = 2 * (PAIRS // 2) + 1 if outs else 0
            span = pl.ds(done, 2 * a + 1 - done)
            outs.append(
                pltpu.make_async_copy(
                    out_buf.at[span], out_hbm.at[out_hbm.shape[0] - 1, span], out_sem.at[len(outs)]
                )
            )
            outs[-1].start()
    for copy in outs:
        copy.wait()


def lagged(place, fan, partner, scale, out_dtype, rounds):
    count, rows = fan.shape[:2]
    channels, length = partner.shape[1:]
    anywhere = pl.BlockSpec(memory_space=pl.ANY)
    buffer = []
    if rounds > 1:
        buffer = [pltpu.VMEM((LAGS, rows, channels), out_dtype), pltpu.SemaphoreType.DMA((2,))]
    return pl.pallas_call(
        functools.partial(lagged_kernel, count, scale),
        out_shape=jax.ShapeDtypeStruct((rounds, LAGS, rows, channels), out_dtype),
        in_specs=[
            pl.BlockSpec(memory_space=pltpu.SMEM),
            anywhere,
            anywhere,
        ],
        out_specs=anywhere if buffer else pl.BlockSpec(memory_space=pltpu.VMEM),
        scratch_shapes=[
            pltpu.VMEM(fan.shape, jnp.bfloat16),
            pltpu.VMEM((2 * channels, length), jnp.bfloat16),
            pltpu.VMEM((channels, LANES), jnp.float32),
            pltpu.VMEM((PAIRS * rows, 2 * channels), jnp.float32),
            pltpu.VMEM((count, channels, length), jnp.bfloat16),
            pltpu.SemaphoreType.DMA((count,)),
            pltpu.SemaphoreType.DMA((count,)),
        ]
        + buffer,
        compiler_params=pltpu.CompilerParams(vmem_limit_bytes=VMEM_BYTES),
        cost_estimate=pl.CostEstimate(
            flops=4 * count * PAIRS * rows * channels * length,
            bytes_accessed=2 * count * channels * length,
            transcendentals=0,
        ),
        name="lagged",
    )(place, fan, partner)


def on_device(raw_strain, band_index, filter_taps):
    channels, length = raw_strain.shape
    count = lax.axis_size("ta")
    rows = channels // count
    scale = 1.0 / math.sqrt(length * count)
    swap = [(0, 1), (1, 0)]
    half, upper, piece = lax.axis_index("zh"), lax.axis_index("cp"), lax.axis_index("ta")

    zero = 0 * piece
    here = jnp.stack([zero, piece % 2, piece, zero + count]).astype(jnp.int32)
    normalized = normalize(raw_strain, band_index, filter_taps, here)
    ring = lax.all_gather(normalized, ("zh", "ta"), axis=0, tiled=False)
    own = lax.all_to_all(normalized.reshape(count, rows, length), "ta", 0, 0)
    guest = lax.ppermute(own, "cp", swap)
    guest_fan, own_fan = fan_of(guest), fan_of(own)

    other = (1 - half) * count
    near = jnp.where(upper == 1, other, half * count)
    place0 = near[None].astype(jnp.int32)
    place1 = other[None].astype(jnp.int32)
    first = lagged(place0, guest_fan, ring, scale, jnp.bfloat16, 1)
    place1, first = lax.optimization_barrier((place1, first))
    first = lax.ppermute(first, "cp", swap)
    result = lagged(place1, own_fan, ring, scale, jnp.float32, ROUNDS)
    return lax.dynamic_update_slice_in_dim(result, first.astype(jnp.float32), 0, 0)


def solution(mesh):
    blocks, slices = mesh.devices.shape
    axes = ("zh", "cp", "col", "ta")
    parts = Mesh(mesh.devices.reshape(2, 2, blocks // 4, slices), axes)
    channel_axes = axes[:3]
    return jax.shard_map(
        on_device,
        mesh=parts,
        in_specs=(P(channel_axes, "ta"), P(channel_axes), P()),
        out_specs=P(None, None, axes, None),
        check_vma=False,
    )
```

```python
import functools
import math

import jax
import jax.numpy as jnp
from jax import lax
from jax.experimental import pallas as pl
from jax.experimental.pallas import tpu as pltpu
from jax.sharding import Mesh
from jax.sharding import PartitionSpec as P

HF = 16
TAPS = 33
NBANDS = 4
LAGH = 32
LAGS = 65
PAIRS = LAGH + 1
LANES = 128
AHEAD = 3
ROUNDS = 2
CHUNK = 64
VMEM_BYTES = 52 * 1024 * 1024


def to_neighbours(on_chip, off_chip):
    count = lax.axis_size("ta")
    inner = [(i, i ^ 1) for i in range(count)]
    outer = [(i, i - 1 + 2 * (i % 2)) for i in range(1, count - 1)]
    off_chip = lax.ppermute(off_chip, "ta", outer)
    return lax.ppermute(on_chip, "ta", inner), off_chip


def filter_kernel(
    place_ref, coeff_ref, tall_ref, inner_ref, outer_ref, out_ref, total_ref, lanes_ref, off_chip_ref, tall, wide
):
    length, channels = tall_ref.shape
    tiles = length // LANES
    first_core = place_ref[1] == 0
    tall[:HF] = jnp.where(first_core, outer_ref[...], inner_ref[...]).T[LANES - HF :]
    tall[HF : HF + length] = tall_ref[...]
    tall[HF + length :] = jnp.where(first_core, inner_ref[...], outer_ref[...]).T[:HF]

    def chunk(i, carry):
        base = pl.multiple_of(i * CHUNK, CHUNK)
        total = jnp.zeros((CHUNK, channels), jnp.float32)
        for k in range(TAPS):
            total = total + coeff_ref[k : k + 1, :] * tall[pl.ds(base + k, CHUNK), :]
        wide[pl.ds(base, CHUNK), :] = total
        return carry

    lax.fori_loop(0, length // CHUNK, chunk, 0)
    lane_total = jnp.zeros((channels, LANES), jnp.float32)
    for r in range(tiles):
        piece = wide[pl.ds(r, LANES, stride=tiles), :].T
        out_ref[:, r * LANES : (r + 1) * LANES] = piece
        lane_total = lane_total + jnp.abs(piece)
    row = lax.broadcasted_iota(jnp.int32, (LANES, LANES), 0)
    col = lax.broadcasted_iota(jnp.int32, (LANES, LANES), 1)
    earlier = jnp.dot(
        lane_total,
        (row < col).astype(jnp.float32),
        precision=lax.Precision.HIGHEST,
        preferred_element_type=jnp.float32,
    )
    total = jnp.broadcast_to((earlier + lane_total)[:, LANES - 1 :], (channels, LANES))
    total_ref[...] = total

    later = total - earlier - lane_total
    lanes_ref[...] = jnp.where(first_core, later, earlier)

    @pl.when(first_core)
    def _():
        pack(off_chip_ref, out_ref, earlier, range(tiles))

    @pl.when(jnp.logical_not(first_core))
    def _():
        pack(off_chip_ref, out_ref, later, range(tiles - 1, -1, -1))


def pack(ref, filtered_ref, lanes_sum, order):
    channels, length = filtered_ref.shape
    inner = jnp.zeros((channels, LANES), jnp.float32)
    for r in order:
        cols = slice(r * LANES, (r + 1) * LANES)
        inner = inner + jnp.abs(filtered_ref[:, cols])
        ref[:, cols] = inner.astype(jnp.bfloat16)
    rest = lanes_sum
    for i in range(ref.shape[1] // LANES - len(order)):
        term = rest.astype(jnp.bfloat16)
        ref[:, length + i * LANES : length + (i + 1) * LANES] = term
        rest = rest - term.astype(jnp.float32)


def pack_kernel(place_ref, filtered_ref, lanes_ref, on_chip_ref):
    tiles = filtered_ref.shape[1] // LANES
    first_core = place_ref[1] == 0

    @pl.when(first_core)
    def _():
        pack(on_chip_ref, filtered_ref, lanes_ref[...], range(tiles - 1, -1, -1))

    @pl.when(jnp.logical_not(first_core))
    def _():
        pack(on_chip_ref, filtered_ref, lanes_ref[...], range(tiles))


def lane_terms(ref, length):
    return sum(
        ref[:, start : start + LANES].astype(jnp.float32)
        for start in range(length, ref.shape[1], LANES)
    )


def prepare_kernel(place_ref, filtered_ref, total_ref, on_chip_ref, top_ref, bottom_ref):
    length = filtered_ref.shape[1]
    tiles = length // LANES
    base = total_ref[...] + lane_terms(on_chip_ref, length)
    lane = lax.broadcasted_iota(jnp.int32, (1, LANES), 1)
    for r in range(tiles):
        cols = slice(r * LANES, (r + 1) * LANES)
        time = place_ref[2] * length + tiles * lane + r
        upper = jnp.minimum(time + length, length * place_ref[3] - 1) + 1
        lower = jnp.maximum(time - length, 0)
        counted = (upper - lower).astype(jnp.float32)
        top_ref[:, cols] = filtered_ref[:, cols] * counted
        bottom_ref[:, cols] = base + on_chip_ref[:, cols].astype(jnp.float32) + 1e-06 * counted


def normalize_kernel(top_ref, bottom_ref, off_chip_ref, out_ref):
    length = top_ref.shape[1]
    base = lane_terms(off_chip_ref, length)
    for r in range(length // LANES):
        cols = slice(r * LANES, (r + 1) * LANES)
        bottom = bottom_ref[:, cols] + (base + off_chip_ref[:, cols].astype(jnp.float32))
        out_ref[:, cols] = (top_ref[:, cols] / bottom).astype(jnp.bfloat16)


def normalize(raw, band_index, filter_taps, place):
    channels, length = raw.shape
    first_core = place[1] == 0
    low, high = raw[:, :LANES], raw[:, length - LANES :]
    inner, outer = to_neighbours(
        jnp.where(first_core, high, low), jnp.where(first_core, low, high)
    )
    chosen = (jnp.arange(NBANDS, dtype=jnp.int32)[:, None] == band_index[None, :]).astype(jnp.float32)
    coeff = lax.dot_general(
        filter_taps,
        chosen,
        (((0,), (0,)), ((), ())),
        precision=lax.Precision.HIGHEST,
        preferred_element_type=jnp.float32,
    )
    vmem = pl.BlockSpec(memory_space=pltpu.VMEM)
    smem = pl.BlockSpec(memory_space=pltpu.SMEM)
    packed = jax.ShapeDtypeStruct((channels, length + 3 * LANES), jnp.bfloat16)
    lanes = jax.ShapeDtypeStruct((channels, LANES), jnp.float32)
    filtered, total, part, off_chip = pl.pallas_call(
        filter_kernel,
        out_shape=(
            jax.ShapeDtypeStruct((channels, length), jnp.float32),
            lanes,
            lanes,
            packed,
        ),
        in_specs=[smem] + [vmem] * 4,
        out_specs=(vmem,) * 4,
        scratch_shapes=[
            pltpu.VMEM((length + 2 * HF, channels), jnp.float32),
            pltpu.VMEM((length, channels), jnp.float32),
        ],
        compiler_params=pltpu.CompilerParams(vmem_limit_bytes=24 * 1024 * 1024),
        name="filter",
    )(place, coeff, lax.optimization_barrier(raw).T, inner, outer)
    on_chip = pl.pallas_call(
        pack_kernel,
        out_shape=jax.ShapeDtypeStruct((channels, length + 2 * LANES), jnp.bfloat16),
        in_specs=[smem, vmem, vmem],
        out_specs=vmem,
        compiler_params=pltpu.CompilerParams(vmem_limit_bytes=24 * 1024 * 1024),
        cost_estimate=pl.CostEstimate(
            flops=2 * channels * length, bytes_accessed=16 * channels * length, transcendentals=0
        ),
        name="pack",
    )(place, filtered, part)
    on_chip, off_chip = to_neighbours(on_chip, off_chip)
    whole = jax.ShapeDtypeStruct((channels, length), jnp.float32)
    top, bottom = pl.pallas_call(
        prepare_kernel,
        out_shape=(whole, whole),
        in_specs=[smem] + [vmem] * 3,
        out_specs=(vmem, vmem),
        compiler_params=pltpu.CompilerParams(vmem_limit_bytes=24 * 1024 * 1024),
        cost_estimate=pl.CostEstimate(
            flops=4 * channels * length, bytes_accessed=16 * channels * length, transcendentals=0
        ),
        name="prepare",
    )(place, filtered, total, on_chip)
    return pl.pallas_call(
        normalize_kernel,
        out_shape=jax.ShapeDtypeStruct((channels, length), jnp.bfloat16),
        in_specs=[vmem] * 3,
        out_specs=vmem,
        compiler_params=pltpu.CompilerParams(vmem_limit_bytes=24 * 1024 * 1024),
        name="normalize",
    )(top, bottom, off_chip)


def fan_kernel(row_ref, out_ref):
    count, rows, length = row_ref.shape
    tiles = length // LANES
    reach = -(-LAGH // tiles)
    lane = lax.broadcasted_iota(jnp.int32, (rows, length), 1) % LANES

    def body(step, unused):
        inside = row_ref[step].astype(jnp.float32)
        left = row_ref[jnp.maximum(step - 1, 0)].astype(jnp.float32)
        left = jnp.where(step > 0, left, 0.0)
        right = row_ref[jnp.minimum(step + 1, count - 1)].astype(jnp.float32)
        right = jnp.where(step < count - 1, right, 0.0)
        for j in range(-reach, reach + 1):
            if j < 0:
                mixed = jnp.where(lane >= LANES + j, left, inside)
            else:
                mixed = jnp.where(lane < j, right, inside)
            for r in range(tiles):
                tile = mixed[:, r * LANES : (r + 1) * LANES]
                if j != 0:
                    tile = pltpu.roll(tile, (-j) % LANES, 1)
                at = (j + reach) * tiles + r
                out_ref[step, :, at * LANES : (at + 1) * LANES] = tile.astype(jnp.bfloat16)
        return unused

    lax.fori_loop(0, count, body, 0)


def fan_of(own_rows):
    count, rows, length = own_rows.shape
    tiles = length // LANES
    fan_tiles = (2 * -(-LAGH // tiles) + 1) * tiles
    vmem = pl.BlockSpec(memory_space=pltpu.VMEM)
    return pl.pallas_call(
        fan_kernel,
        out_shape=jax.ShapeDtypeStruct((count, rows, fan_tiles * LANES), jnp.bfloat16),
        in_specs=[vmem],
        out_specs=vmem,
        compiler_params=pltpu.CompilerParams(vmem_limit_bytes=24 * 1024 * 1024),
        cost_estimate=pl.CostEstimate(
            flops=20 * count * rows * fan_tiles * LANES,
            bytes_accessed=2 * count * rows * fan_tiles * LANES,
            transcendentals=0,
        ),
        name="fan",
    )(own_rows)


def lagged_kernel(
    count, scale, place_ref, fan_hbm, part_hbm, out_hbm, fan_buf, both, carry, acc, part_buf, fan_sem, part_sem, *buffer
):
    out_buf, out_sem = buffer if buffer else (out_hbm.at[0], None)
    rows = fan_buf.shape[1]
    channels, length = part_buf.shape[1:]
    tiles = length // LANES
    lead = -(-LAGH // tiles) * tiles + LAGH

    def part_copy(t):
        return pltpu.make_async_copy(
            part_hbm.at[place_ref[0] + t], part_buf.at[t], part_sem.at[t]
        )

    def fan_copy(t):
        return pltpu.make_async_copy(fan_hbm.at[t], fan_buf.at[t], fan_sem.at[t])

    for t in range(AHEAD):
        part_copy(t).start()
        fan_copy(t).start()
    acc[...] = jnp.zeros_like(acc)
    carry[...] = jnp.zeros_like(carry)
    part_lane = lax.broadcasted_iota(jnp.int32, (channels, LANES), 1)

    def moved(step, width, offset):
        return jnp.concatenate(
            [
                fan_buf[
                    step, :, (lead - 2 * a + offset) * LANES : (lead - 2 * a + offset + width) * LANES
                ]
                for a in range(PAIRS)
            ],
            axis=0,
        )

    def body(step, unused):
        @pl.when(step + AHEAD < count)
        def _():
            part_copy(step + AHEAD).start()
            fan_copy(step + AHEAD).start()

        part_copy(step).wait()
        both[:channels] = part_buf[step]
        both[channels:, LANES:] = part_buf[step, :, : length - LANES]
        final = part_buf[step, :, length - LANES :].astype(jnp.float32)
        late = pltpu.roll(jnp.where(part_lane == LANES - 1, carry[...], final), 1, 1)
        both[channels:, :LANES] = late.astype(jnp.bfloat16)
        carry[...] = final
        fan_copy(step).wait()
        acc[...] += lax.dot_general(
            moved(step, tiles, 0),
            both[...],
            (((1,), (1,)), ((), ())),
            preferred_element_type=jnp.float32,
        )
        return unused

    lax.fori_loop(0, count, body, 0)
    tail = jnp.where(part_lane == LANES - 1, carry[...], 0.0).astype(jnp.bfloat16)
    acc[:, channels:] += lax.dot_general(
        moved(count - 1, 1, tiles),
        tail,
        (((1,), (1,)), ((), ())),
        preferred_element_type=jnp.float32,
    )
    outs = []
    for a in range(PAIRS):
        block = acc[a * rows : (a + 1) * rows] * scale
        out_buf[2 * a] = block[:, :channels].astype(out_buf.dtype)
        if a > 0:
            out_buf[2 * a - 1] = block[:, channels:].astype(out_buf.dtype)
        if buffer and a in (PAIRS // 2, PAIRS - 1):
            done = 2 * (PAIRS // 2) + 1 if outs else 0
            span = pl.ds(done, 2 * a + 1 - done)
            outs.append(
                pltpu.make_async_copy(
                    out_buf.at[span], out_hbm.at[out_hbm.shape[0] - 1, span], out_sem.at[len(outs)]
                )
            )
            outs[-1].start()
    for copy in outs:
        copy.wait()


def lagged(place, fan, partner, scale, out_dtype, rounds):
    count, rows = fan.shape[:2]
    channels, length = partner.shape[1:]
    anywhere = pl.BlockSpec(memory_space=pl.ANY)
    buffer = []
    if rounds > 1:
        buffer = [pltpu.VMEM((LAGS, rows, channels), out_dtype), pltpu.SemaphoreType.DMA((2,))]
    return pl.pallas_call(
        functools.partial(lagged_kernel, count, scale),
        out_shape=jax.ShapeDtypeStruct((rounds, LAGS, rows, channels), out_dtype),
        in_specs=[
            pl.BlockSpec(memory_space=pltpu.SMEM),
            anywhere,
            anywhere,
        ],
        out_specs=anywhere if buffer else pl.BlockSpec(memory_space=pltpu.VMEM),
        scratch_shapes=[
            pltpu.VMEM(fan.shape, jnp.bfloat16),
            pltpu.VMEM((2 * channels, length), jnp.bfloat16),
            pltpu.VMEM((channels, LANES), jnp.float32),
            pltpu.VMEM((PAIRS * rows, 2 * channels), jnp.float32),
            pltpu.VMEM((count, channels, length), jnp.bfloat16),
            pltpu.SemaphoreType.DMA((count,)),
            pltpu.SemaphoreType.DMA((count,)),
        ]
        + buffer,
        compiler_params=pltpu.CompilerParams(vmem_limit_bytes=VMEM_BYTES),
        cost_estimate=pl.CostEstimate(
            flops=4 * count * PAIRS * rows * channels * length,
            bytes_accessed=2 * count * channels * length,
            transcendentals=0,
        ),
        name="lagged",
    )(place, fan, partner)


def on_device(raw_strain, band_index, filter_taps):
    channels, length = raw_strain.shape
    count = lax.axis_size("ta")
    rows = channels // count
    scale = 1.0 / math.sqrt(length * count)
    swap = [(0, 1), (1, 0)]
    half, upper, piece = lax.axis_index("zh"), lax.axis_index("cp"), lax.axis_index("ta")

    zero = 0 * piece
    here = jnp.stack([zero, piece % 2, piece, zero + count]).astype(jnp.int32)
    normalized = normalize(raw_strain, band_index, filter_taps, here)
    ring = lax.all_gather(normalized, ("zh", "ta"), axis=0, tiled=False)
    own = lax.all_to_all(normalized.reshape(count, rows, length), "ta", 0, 0)
    guest = lax.ppermute(own, "cp", swap)
    guest_fan, own_fan = fan_of(guest), fan_of(own)

    other = (1 - half) * count
    near = jnp.where(upper == 1, other, half * count)
    place0 = near[None].astype(jnp.int32)
    place1 = other[None].astype(jnp.int32)
    first = lagged(place0, guest_fan, ring, scale, jnp.bfloat16, 1)
    place1, first = lax.optimization_barrier((place1, first))
    first = lax.ppermute(first, "cp", swap)
    result = lagged(place1, own_fan, ring, scale, jnp.float32, ROUNDS)
    return lax.dynamic_update_slice_in_dim(result, first.astype(jnp.float32), 0, 0)


def solution(mesh):
    blocks, slices = mesh.devices.shape
    axes = ("zh", "cp", "col", "ta")
    parts = Mesh(mesh.devices.reshape(2, 2, blocks // 4, slices), axes)
    channel_axes = axes[:3]
    return jax.shard_map(
        on_device,
        mesh=parts,
        in_specs=(P(channel_axes, "ta"), P(channel_axes), P()),
        out_specs=P(None, None, axes, None),
        check_vma=False,
    )
```

```python
import functools
import math

import jax
import jax.numpy as jnp
from jax import lax
from jax.experimental import pallas as pl
from jax.experimental.pallas import tpu as pltpu
from jax.sharding import Mesh
from jax.sharding import PartitionSpec as P

HF = 16
TAPS = 33
NBANDS = 4
LAGH = 32
LAGS = 65
PAIRS = LAGH + 1
LANES = 128
AHEAD = 3
ROUNDS = 2
CHUNK = 192
VMEM_BYTES = 52 * 1024 * 1024


def to_neighbours(on_chip, off_chip):
    count = lax.axis_size("ta")
    inner = [(i, i ^ 1) for i in range(count)]
    outer = [(i, i - 1 + 2 * (i % 2)) for i in range(1, count - 1)]
    off_chip = lax.ppermute(off_chip, "ta", outer)
    return lax.ppermute(on_chip, "ta", inner), off_chip


def filter_kernel(
    place_ref, coeff_ref, tall_ref, inner_ref, outer_ref, out_ref, total_ref, lanes_ref, off_chip_ref, tall, wide
):
    length, channels = tall_ref.shape
    tiles = length // LANES
    first_core = place_ref[1] == 0
    tall[:HF] = jnp.where(first_core, outer_ref[...], inner_ref[...]).T[LANES - HF :]
    tall[HF : HF + length] = tall_ref[...]
    tall[HF + length :] = jnp.where(first_core, inner_ref[...], outer_ref[...]).T[:HF]

    def chunk(i, carry):
        base = pl.multiple_of(i * CHUNK, CHUNK)
        total = jnp.zeros((CHUNK, channels), jnp.float32)
        for k in range(TAPS):
            total = total + coeff_ref[k : k + 1, :] * tall[pl.ds(base + k, CHUNK), :]
        wide[pl.ds(base, CHUNK), :] = total
        return carry

    lax.fori_loop(0, length // CHUNK, chunk, 0)
    lane_total = jnp.zeros((channels, LANES), jnp.float32)
    for r in range(tiles):
        piece = wide[pl.ds(r, LANES, stride=tiles), :].T
        out_ref[:, r * LANES : (r + 1) * LANES] = piece
        lane_total = lane_total + jnp.abs(piece)
    row = lax.broadcasted_iota(jnp.int32, (LANES, LANES), 0)
    col = lax.broadcasted_iota(jnp.int32, (LANES, LANES), 1)
    earlier = jnp.dot(
        lane_total,
        (row < col).astype(jnp.float32),
        precision=lax.Precision.HIGHEST,
        preferred_element_type=jnp.float32,
    )
    total = jnp.broadcast_to((earlier + lane_total)[:, LANES - 1 :], (channels, LANES))
    total_ref[...] = total

    later = total - earlier - lane_total
    lanes_ref[...] = jnp.where(first_core, later, earlier)

    @pl.when(first_core)
    def _():
        pack(off_chip_ref, out_ref, earlier, range(tiles))

    @pl.when(jnp.logical_not(first_core))
    def _():
        pack(off_chip_ref, out_ref, later, range(tiles - 1, -1, -1))


def pack(ref, filtered_ref, lanes_sum, order):
    channels, length = filtered_ref.shape
    inner = jnp.zeros((channels, LANES), jnp.float32)
    for r in order:
        cols = slice(r * LANES, (r + 1) * LANES)
        inner = inner + jnp.abs(filtered_ref[:, cols])
        ref[:, cols] = inner.astype(jnp.bfloat16)
    rest = lanes_sum
    for i in range(ref.shape[1] // LANES - len(order)):
        term = rest.astype(jnp.bfloat16)
        ref[:, length + i * LANES : length + (i + 1) * LANES] = term
        rest = rest - term.astype(jnp.float32)


def pack_kernel(place_ref, filtered_ref, lanes_ref, on_chip_ref):
    tiles = filtered_ref.shape[1] // LANES
    first_core = place_ref[1] == 0

    @pl.when(first_core)
    def _():
        pack(on_chip_ref, filtered_ref, lanes_ref[...], range(tiles - 1, -1, -1))

    @pl.when(jnp.logical_not(first_core))
    def _():
        pack(on_chip_ref, filtered_ref, lanes_ref[...], range(tiles))


def lane_terms(ref, length):
    return sum(
        ref[:, start : start + LANES].astype(jnp.float32)
        for start in range(length, ref.shape[1], LANES)
    )


def prepare_kernel(place_ref, filtered_ref, total_ref, on_chip_ref, top_ref, bottom_ref):
    length = filtered_ref.shape[1]
    tiles = length // LANES
    base = total_ref[...] + lane_terms(on_chip_ref, length)
    lane = lax.broadcasted_iota(jnp.int32, (1, LANES), 1)
    for r in range(tiles):
        cols = slice(r * LANES, (r + 1) * LANES)
        time = place_ref[2] * length + tiles * lane + r
        upper = jnp.minimum(time + length, length * place_ref[3] - 1) + 1
        lower = jnp.maximum(time - length, 0)
        counted = (upper - lower).astype(jnp.float32)
        top_ref[:, cols] = filtered_ref[:, cols] * counted
        bottom_ref[:, cols] = base + on_chip_ref[:, cols].astype(jnp.float32) + 1e-06 * counted


def normalize_kernel(top_ref, bottom_ref, off_chip_ref, out_ref):
    length = top_ref.shape[1]
    base = lane_terms(off_chip_ref, length)
    for r in range(length // LANES):
        cols = slice(r * LANES, (r + 1) * LANES)
        bottom = bottom_ref[:, cols] + (base + off_chip_ref[:, cols].astype(jnp.float32))
        out_ref[:, cols] = (top_ref[:, cols] / bottom).astype(jnp.bfloat16)


def normalize(raw, band_index, filter_taps, place):
    channels, length = raw.shape
    first_core = place[1] == 0
    low, high = raw[:, :LANES], raw[:, length - LANES :]
    inner, outer = to_neighbours(
        jnp.where(first_core, high, low), jnp.where(first_core, low, high)
    )
    chosen = (jnp.arange(NBANDS, dtype=jnp.int32)[:, None] == band_index[None, :]).astype(jnp.float32)
    coeff = lax.dot_general(
        filter_taps,
        chosen,
        (((0,), (0,)), ((), ())),
        precision=lax.Precision.HIGHEST,
        preferred_element_type=jnp.float32,
    )
    vmem = pl.BlockSpec(memory_space=pltpu.VMEM)
    smem = pl.BlockSpec(memory_space=pltpu.SMEM)
    packed = jax.ShapeDtypeStruct((channels, length + 3 * LANES), jnp.bfloat16)
    lanes = jax.ShapeDtypeStruct((channels, LANES), jnp.float32)
    filtered, total, part, off_chip = pl.pallas_call(
        filter_kernel,
        out_shape=(
            jax.ShapeDtypeStruct((channels, length), jnp.float32),
            lanes,
            lanes,
            packed,
        ),
        in_specs=[smem] + [vmem] * 4,
        out_specs=(vmem,) * 4,
        scratch_shapes=[
            pltpu.VMEM((length + 2 * HF, channels), jnp.float32),
            pltpu.VMEM((length, channels), jnp.float32),
        ],
        compiler_params=pltpu.CompilerParams(vmem_limit_bytes=24 * 1024 * 1024),
        name="filter",
    )(place, coeff, lax.optimization_barrier(raw).T, inner, outer)
    on_chip = pl.pallas_call(
        pack_kernel,
        out_shape=jax.ShapeDtypeStruct((channels, length + 2 * LANES), jnp.bfloat16),
        in_specs=[smem, vmem, vmem],
        out_specs=vmem,
        compiler_params=pltpu.CompilerParams(vmem_limit_bytes=24 * 1024 * 1024),
        cost_estimate=pl.CostEstimate(
            flops=2 * channels * length, bytes_accessed=16 * channels * length, transcendentals=0
        ),
        name="pack",
    )(place, filtered, part)
    on_chip, off_chip = to_neighbours(on_chip, off_chip)
    whole = jax.ShapeDtypeStruct((channels, length), jnp.float32)
    top, bottom = pl.pallas_call(
        prepare_kernel,
        out_shape=(whole, whole),
        in_specs=[smem] + [vmem] * 3,
        out_specs=(vmem, vmem),
        compiler_params=pltpu.CompilerParams(vmem_limit_bytes=24 * 1024 * 1024),
        cost_estimate=pl.CostEstimate(
            flops=4 * channels * length, bytes_accessed=16 * channels * length, transcendentals=0
        ),
        name="prepare",
    )(place, filtered, total, on_chip)
    return pl.pallas_call(
        normalize_kernel,
        out_shape=jax.ShapeDtypeStruct((channels, length), jnp.bfloat16),
        in_specs=[vmem] * 3,
        out_specs=vmem,
        compiler_params=pltpu.CompilerParams(vmem_limit_bytes=24 * 1024 * 1024),
        name="normalize",
    )(top, bottom, off_chip)


def fan_kernel(row_ref, out_ref):
    count, rows, length = row_ref.shape
    tiles = length // LANES
    reach = -(-LAGH // tiles)
    lane = lax.broadcasted_iota(jnp.int32, (rows, length), 1) % LANES

    def body(step, unused):
        inside = row_ref[step].astype(jnp.float32)
        left = row_ref[jnp.maximum(step - 1, 0)].astype(jnp.float32)
        left = jnp.where(step > 0, left, 0.0)
        right = row_ref[jnp.minimum(step + 1, count - 1)].astype(jnp.float32)
        right = jnp.where(step < count - 1, right, 0.0)
        for j in range(-reach, reach + 1):
            if j < 0:
                mixed = jnp.where(lane >= LANES + j, left, inside)
            else:
                mixed = jnp.where(lane < j, right, inside)
            for r in range(tiles):
                tile = mixed[:, r * LANES : (r + 1) * LANES]
                if j != 0:
                    tile = pltpu.roll(tile, (-j) % LANES, 1)
                at = (j + reach) * tiles + r
                out_ref[step, :, at * LANES : (at + 1) * LANES] = tile.astype(jnp.bfloat16)
        return unused

    lax.fori_loop(0, count, body, 0)


def fan_of(own_rows):
    count, rows, length = own_rows.shape
    tiles = length // LANES
    fan_tiles = (2 * -(-LAGH // tiles) + 1) * tiles
    vmem = pl.BlockSpec(memory_space=pltpu.VMEM)
    return pl.pallas_call(
        fan_kernel,
        out_shape=jax.ShapeDtypeStruct((count, rows, fan_tiles * LANES), jnp.bfloat16),
        in_specs=[vmem],
        out_specs=vmem,
        compiler_params=pltpu.CompilerParams(vmem_limit_bytes=24 * 1024 * 1024),
        cost_estimate=pl.CostEstimate(
            flops=20 * count * rows * fan_tiles * LANES,
            bytes_accessed=2 * count * rows * fan_tiles * LANES,
            transcendentals=0,
        ),
        name="fan",
    )(own_rows)


def lagged_kernel(
    count, scale, place_ref, fan_hbm, part_hbm, out_hbm, fan_buf, both, carry, acc, part_buf, fan_sem, part_sem, *buffer
):
    out_buf, out_sem = buffer if buffer else (out_hbm.at[0], None)
    rows = fan_buf.shape[1]
    channels, length = part_buf.shape[1:]
    tiles = length // LANES
    lead = -(-LAGH // tiles) * tiles + LAGH

    def part_copy(t):
        return pltpu.make_async_copy(
            part_hbm.at[place_ref[0] + t], part_buf.at[t], part_sem.at[t]
        )

    def fan_copy(t):
        return pltpu.make_async_copy(fan_hbm.at[t], fan_buf.at[t], fan_sem.at[t])

    for t in range(AHEAD):
        part_copy(t).start()
        fan_copy(t).start()
    acc[...] = jnp.zeros_like(acc)
    carry[...] = jnp.zeros_like(carry)
    part_lane = lax.broadcasted_iota(jnp.int32, (channels, LANES), 1)

    def moved(step, width, offset):
        return jnp.concatenate(
            [
                fan_buf[
                    step, :, (lead - 2 * a + offset) * LANES : (lead - 2 * a + offset + width) * LANES
                ]
                for a in range(PAIRS)
            ],
            axis=0,
        )

    def body(step, unused):
        @pl.when(step + AHEAD < count)
        def _():
            part_copy(step + AHEAD).start()
            fan_copy(step + AHEAD).start()

        part_copy(step).wait()
        both[:channels] = part_buf[step]
        both[channels:, LANES:] = part_buf[step, :, : length - LANES]
        final = part_buf[step, :, length - LANES :].astype(jnp.float32)
        late = pltpu.roll(jnp.where(part_lane == LANES - 1, carry[...], final), 1, 1)
        both[channels:, :LANES] = late.astype(jnp.bfloat16)
        carry[...] = final
        fan_copy(step).wait()
        acc[...] += lax.dot_general(
            moved(step, tiles, 0),
            both[...],
            (((1,), (1,)), ((), ())),
            preferred_element_type=jnp.float32,
        )
        return unused

    lax.fori_loop(0, count, body, 0)
    tail = jnp.where(part_lane == LANES - 1, carry[...], 0.0).astype(jnp.bfloat16)
    acc[:, channels:] += lax.dot_general(
        moved(count - 1, 1, tiles),
        tail,
        (((1,), (1,)), ((), ())),
        preferred_element_type=jnp.float32,
    )
    outs = []
    for a in range(PAIRS):
        block = acc[a * rows : (a + 1) * rows] * scale
        out_buf[2 * a] = block[:, :channels].astype(out_buf.dtype)
        if a > 0:
            out_buf[2 * a - 1] = block[:, channels:].astype(out_buf.dtype)
        if buffer and a in (PAIRS // 2, PAIRS - 1):
            done = 2 * (PAIRS // 2) + 1 if outs else 0
            span = pl.ds(done, 2 * a + 1 - done)
            outs.append(
                pltpu.make_async_copy(
                    out_buf.at[span], out_hbm.at[out_hbm.shape[0] - 1, span], out_sem.at[len(outs)]
                )
            )
            outs[-1].start()
    for copy in outs:
        copy.wait()


def lagged(place, fan, partner, scale, out_dtype, rounds):
    count, rows = fan.shape[:2]
    channels, length = partner.shape[1:]
    anywhere = pl.BlockSpec(memory_space=pl.ANY)
    buffer = []
    if rounds > 1:
        buffer = [pltpu.VMEM((LAGS, rows, channels), out_dtype), pltpu.SemaphoreType.DMA((2,))]
    return pl.pallas_call(
        functools.partial(lagged_kernel, count, scale),
        out_shape=jax.ShapeDtypeStruct((rounds, LAGS, rows, channels), out_dtype),
        in_specs=[
            pl.BlockSpec(memory_space=pltpu.SMEM),
            anywhere,
            anywhere,
        ],
        out_specs=anywhere if buffer else pl.BlockSpec(memory_space=pltpu.VMEM),
        scratch_shapes=[
            pltpu.VMEM(fan.shape, jnp.bfloat16),
            pltpu.VMEM((2 * channels, length), jnp.bfloat16),
            pltpu.VMEM((channels, LANES), jnp.float32),
            pltpu.VMEM((PAIRS * rows, 2 * channels), jnp.float32),
            pltpu.VMEM((count, channels, length), jnp.bfloat16),
            pltpu.SemaphoreType.DMA((count,)),
            pltpu.SemaphoreType.DMA((count,)),
        ]
        + buffer,
        compiler_params=pltpu.CompilerParams(vmem_limit_bytes=VMEM_BYTES),
        cost_estimate=pl.CostEstimate(
            flops=4 * count * PAIRS * rows * channels * length,
            bytes_accessed=2 * count * channels * length,
            transcendentals=0,
        ),
        name="lagged",
    )(place, fan, partner)


def on_device(raw_strain, band_index, filter_taps):
    channels, length = raw_strain.shape
    count = lax.axis_size("ta")
    rows = channels // count
    scale = 1.0 / math.sqrt(length * count)
    swap = [(0, 1), (1, 0)]
    half, upper, piece = lax.axis_index("zh"), lax.axis_index("cp"), lax.axis_index("ta")

    zero = 0 * piece
    here = jnp.stack([zero, piece % 2, piece, zero + count]).astype(jnp.int32)
    normalized = normalize(raw_strain, band_index, filter_taps, here)
    ring = lax.all_gather(normalized, ("zh", "ta"), axis=0, tiled=False)
    own = lax.all_to_all(normalized.reshape(count, rows, length), "ta", 0, 0)
    guest = lax.ppermute(own, "cp", swap)
    guest_fan, own_fan = fan_of(guest), fan_of(own)

    other = (1 - half) * count
    near = jnp.where(upper == 1, other, half * count)
    place0 = near[None].astype(jnp.int32)
    place1 = other[None].astype(jnp.int32)
    first = lagged(place0, guest_fan, ring, scale, jnp.bfloat16, 1)
    place1, first = lax.optimization_barrier((place1, first))
    first = lax.ppermute(first, "cp", swap)
    result = lagged(place1, own_fan, ring, scale, jnp.float32, ROUNDS)
    return lax.dynamic_update_slice_in_dim(result, first.astype(jnp.float32), 0, 0)


def solution(mesh):
    blocks, slices = mesh.devices.shape
    axes = ("zh", "cp", "col", "ta")
    parts = Mesh(mesh.devices.reshape(2, 2, blocks // 4, slices), axes)
    channel_axes = axes[:3]
    return jax.shard_map(
        on_device,
        mesh=parts,
        in_specs=(P(channel_axes, "ta"), P(channel_axes), P()),
        out_specs=P(None, None, axes, None),
        check_vma=False,
    )
```

```python
import functools
import math

import jax
import jax.numpy as jnp
from jax import lax
from jax.experimental import pallas as pl
from jax.experimental.pallas import tpu as pltpu
from jax.sharding import Mesh
from jax.sharding import PartitionSpec as P

HF = 16
TAPS = 33
NBANDS = 4
LAGH = 32
LAGS = 65
PAIRS = LAGH + 1
LANES = 128
AHEAD = 3
ROUNDS = 2
CHUNK = 384
VMEM_BYTES = 52 * 1024 * 1024


def to_neighbours(on_chip, off_chip):
    count = lax.axis_size("ta")
    inner = [(i, i ^ 1) for i in range(count)]
    outer = [(i, i - 1 + 2 * (i % 2)) for i in range(1, count - 1)]
    off_chip = lax.ppermute(off_chip, "ta", outer)
    return lax.ppermute(on_chip, "ta", inner), off_chip


def filter_kernel(
    place_ref, coeff_ref, tall_ref, inner_ref, outer_ref, out_ref, total_ref, lanes_ref, off_chip_ref, tall, wide
):
    length, channels = tall_ref.shape
    tiles = length // LANES
    first_core = place_ref[1] == 0
    tall[:HF] = jnp.where(first_core, outer_ref[...], inner_ref[...]).T[LANES - HF :]
    tall[HF : HF + length] = tall_ref[...]
    tall[HF + length :] = jnp.where(first_core, inner_ref[...], outer_ref[...]).T[:HF]

    def chunk(i, carry):
        base = pl.multiple_of(i * CHUNK, CHUNK)
        total = jnp.zeros((CHUNK, channels), jnp.float32)
        for k in range(TAPS):
            total = total + coeff_ref[k : k + 1, :] * tall[pl.ds(base + k, CHUNK), :]
        wide[pl.ds(base, CHUNK), :] = total
        return carry

    lax.fori_loop(0, length // CHUNK, chunk, 0)
    lane_total = jnp.zeros((channels, LANES), jnp.float32)
    for r in range(tiles):
        piece = wide[pl.ds(r, LANES, stride=tiles), :].T
        out_ref[:, r * LANES : (r + 1) * LANES] = piece
        lane_total = lane_total + jnp.abs(piece)
    row = lax.broadcasted_iota(jnp.int32, (LANES, LANES), 0)
    col = lax.broadcasted_iota(jnp.int32, (LANES, LANES), 1)
    earlier = jnp.dot(
        lane_total,
        (row < col).astype(jnp.float32),
        precision=lax.Precision.HIGHEST,
        preferred_element_type=jnp.float32,
    )
    total = jnp.broadcast_to((earlier + lane_total)[:, LANES - 1 :], (channels, LANES))
    total_ref[...] = total

    later = total - earlier - lane_total
    lanes_ref[...] = jnp.where(first_core, later, earlier)

    @pl.when(first_core)
    def _():
        pack(off_chip_ref, out_ref, earlier, range(tiles))

    @pl.when(jnp.logical_not(first_core))
    def _():
        pack(off_chip_ref, out_ref, later, range(tiles - 1, -1, -1))


def pack(ref, filtered_ref, lanes_sum, order):
    channels, length = filtered_ref.shape
    inner = jnp.zeros((channels, LANES), jnp.float32)
    for r in order:
        cols = slice(r * LANES, (r + 1) * LANES)
        inner = inner + jnp.abs(filtered_ref[:, cols])
        ref[:, cols] = inner.astype(jnp.bfloat16)
    rest = lanes_sum
    for i in range(ref.shape[1] // LANES - len(order)):
        term = rest.astype(jnp.bfloat16)
        ref[:, length + i * LANES : length + (i + 1) * LANES] = term
        rest = rest - term.astype(jnp.float32)


def pack_kernel(place_ref, filtered_ref, lanes_ref, on_chip_ref):
    tiles = filtered_ref.shape[1] // LANES
    first_core = place_ref[1] == 0

    @pl.when(first_core)
    def _():
        pack(on_chip_ref, filtered_ref, lanes_ref[...], range(tiles - 1, -1, -1))

    @pl.when(jnp.logical_not(first_core))
    def _():
        pack(on_chip_ref, filtered_ref, lanes_ref[...], range(tiles))


def lane_terms(ref, length):
    return sum(
        ref[:, start : start + LANES].astype(jnp.float32)
        for start in range(length, ref.shape[1], LANES)
    )


def prepare_kernel(place_ref, filtered_ref, total_ref, on_chip_ref, top_ref, bottom_ref):
    length = filtered_ref.shape[1]
    tiles = length // LANES
    base = total_ref[...] + lane_terms(on_chip_ref, length)
    lane = lax.broadcasted_iota(jnp.int32, (1, LANES), 1)
    for r in range(tiles):
        cols = slice(r * LANES, (r + 1) * LANES)
        time = place_ref[2] * length + tiles * lane + r
        upper = jnp.minimum(time + length, length * place_ref[3] - 1) + 1
        lower = jnp.maximum(time - length, 0)
        counted = (upper - lower).astype(jnp.float32)
        top_ref[:, cols] = filtered_ref[:, cols] * counted
        bottom_ref[:, cols] = base + on_chip_ref[:, cols].astype(jnp.float32) + 1e-06 * counted


def normalize_kernel(top_ref, bottom_ref, off_chip_ref, out_ref):
    length = top_ref.shape[1]
    base = lane_terms(off_chip_ref, length)
    for r in range(length // LANES):
        cols = slice(r * LANES, (r + 1) * LANES)
        bottom = bottom_ref[:, cols] + (base + off_chip_ref[:, cols].astype(jnp.float32))
        out_ref[:, cols] = (top_ref[:, cols] / bottom).astype(jnp.bfloat16)


def normalize(raw, band_index, filter_taps, place):
    channels, length = raw.shape
    first_core = place[1] == 0
    low, high = raw[:, :LANES], raw[:, length - LANES :]
    inner, outer = to_neighbours(
        jnp.where(first_core, high, low), jnp.where(first_core, low, high)
    )
    chosen = (jnp.arange(NBANDS, dtype=jnp.int32)[:, None] == band_index[None, :]).astype(jnp.float32)
    coeff = lax.dot_general(
        filter_taps,
        chosen,
        (((0,), (0,)), ((), ())),
        precision=lax.Precision.HIGHEST,
        preferred_element_type=jnp.float32,
    )
    vmem = pl.BlockSpec(memory_space=pltpu.VMEM)
    smem = pl.BlockSpec(memory_space=pltpu.SMEM)
    packed = jax.ShapeDtypeStruct((channels, length + 3 * LANES), jnp.bfloat16)
    lanes = jax.ShapeDtypeStruct((channels, LANES), jnp.float32)
    filtered, total, part, off_chip = pl.pallas_call(
        filter_kernel,
        out_shape=(
            jax.ShapeDtypeStruct((channels, length), jnp.float32),
            lanes,
            lanes,
            packed,
        ),
        in_specs=[smem] + [vmem] * 4,
        out_specs=(vmem,) * 4,
        scratch_shapes=[
            pltpu.VMEM((length + 2 * HF, channels), jnp.float32),
            pltpu.VMEM((length, channels), jnp.float32),
        ],
        compiler_params=pltpu.CompilerParams(vmem_limit_bytes=24 * 1024 * 1024),
        name="filter",
    )(place, coeff, lax.optimization_barrier(raw).T, inner, outer)
    on_chip = pl.pallas_call(
        pack_kernel,
        out_shape=jax.ShapeDtypeStruct((channels, length + 2 * LANES), jnp.bfloat16),
        in_specs=[smem, vmem, vmem],
        out_specs=vmem,
        compiler_params=pltpu.CompilerParams(vmem_limit_bytes=24 * 1024 * 1024),
        cost_estimate=pl.CostEstimate(
            flops=2 * channels * length, bytes_accessed=16 * channels * length, transcendentals=0
        ),
        name="pack",
    )(place, filtered, part)
    on_chip, off_chip = to_neighbours(on_chip, off_chip)
    whole = jax.ShapeDtypeStruct((channels, length), jnp.float32)
    top, bottom = pl.pallas_call(
        prepare_kernel,
        out_shape=(whole, whole),
        in_specs=[smem] + [vmem] * 3,
        out_specs=(vmem, vmem),
        compiler_params=pltpu.CompilerParams(vmem_limit_bytes=24 * 1024 * 1024),
        cost_estimate=pl.CostEstimate(
            flops=4 * channels * length, bytes_accessed=16 * channels * length, transcendentals=0
        ),
        name="prepare",
    )(place, filtered, total, on_chip)
    return pl.pallas_call(
        normalize_kernel,
        out_shape=jax.ShapeDtypeStruct((channels, length), jnp.bfloat16),
        in_specs=[vmem] * 3,
        out_specs=vmem,
        compiler_params=pltpu.CompilerParams(vmem_limit_bytes=24 * 1024 * 1024),
        name="normalize",
    )(top, bottom, off_chip)


def fan_kernel(row_ref, out_ref):
    count, rows, length = row_ref.shape
    tiles = length // LANES
    reach = -(-LAGH // tiles)
    lane = lax.broadcasted_iota(jnp.int32, (rows, length), 1) % LANES

    def body(step, unused):
        inside = row_ref[step].astype(jnp.float32)
        left = row_ref[jnp.maximum(step - 1, 0)].astype(jnp.float32)
        left = jnp.where(step > 0, left, 0.0)
        right = row_ref[jnp.minimum(step + 1, count - 1)].astype(jnp.float32)
        right = jnp.where(step < count - 1, right, 0.0)
        for j in range(-reach, reach + 1):
            if j < 0:
                mixed = jnp.where(lane >= LANES + j, left, inside)
            else:
                mixed = jnp.where(lane < j, right, inside)
            for r in range(tiles):
                tile = mixed[:, r * LANES : (r + 1) * LANES]
                if j != 0:
                    tile = pltpu.roll(tile, (-j) % LANES, 1)
                at = (j + reach) * tiles + r
                out_ref[step, :, at * LANES : (at + 1) * LANES] = tile.astype(jnp.bfloat16)
        return unused

    lax.fori_loop(0, count, body, 0)


def fan_of(own_rows):
    count, rows, length = own_rows.shape
    tiles = length // LANES
    fan_tiles = (2 * -(-LAGH // tiles) + 1) * tiles
    vmem = pl.BlockSpec(memory_space=pltpu.VMEM)
    return pl.pallas_call(
        fan_kernel,
        out_shape=jax.ShapeDtypeStruct((count, rows, fan_tiles * LANES), jnp.bfloat16),
        in_specs=[vmem],
        out_specs=vmem,
        compiler_params=pltpu.CompilerParams(vmem_limit_bytes=24 * 1024 * 1024),
        cost_estimate=pl.CostEstimate(
            flops=20 * count * rows * fan_tiles * LANES,
            bytes_accessed=2 * count * rows * fan_tiles * LANES,
            transcendentals=0,
        ),
        name="fan",
    )(own_rows)


def lagged_kernel(
    count, scale, place_ref, fan_hbm, part_hbm, out_hbm, fan_buf, both, carry, acc, part_buf, fan_sem, part_sem, *buffer
):
    out_buf, out_sem = buffer if buffer else (out_hbm.at[0], None)
    rows = fan_buf.shape[1]
    channels, length = part_buf.shape[1:]
    tiles = length // LANES
    lead = -(-LAGH // tiles) * tiles + LAGH

    def part_copy(t):
        return pltpu.make_async_copy(
            part_hbm.at[place_ref[0] + t], part_buf.at[t], part_sem.at[t]
        )

    def fan_copy(t):
        return pltpu.make_async_copy(fan_hbm.at[t], fan_buf.at[t], fan_sem.at[t])

    for t in range(AHEAD):
        part_copy(t).start()
        fan_copy(t).start()
    acc[...] = jnp.zeros_like(acc)
    carry[...] = jnp.zeros_like(carry)
    part_lane = lax.broadcasted_iota(jnp.int32, (channels, LANES), 1)

    def moved(step, width, offset):
        return jnp.concatenate(
            [
                fan_buf[
                    step, :, (lead - 2 * a + offset) * LANES : (lead - 2 * a + offset + width) * LANES
                ]
                for a in range(PAIRS)
            ],
            axis=0,
        )

    def body(step, unused):
        @pl.when(step + AHEAD < count)
        def _():
            part_copy(step + AHEAD).start()
            fan_copy(step + AHEAD).start()

        part_copy(step).wait()
        both[:channels] = part_buf[step]
        both[channels:, LANES:] = part_buf[step, :, : length - LANES]
        final = part_buf[step, :, length - LANES :].astype(jnp.float32)
        late = pltpu.roll(jnp.where(part_lane == LANES - 1, carry[...], final), 1, 1)
        both[channels:, :LANES] = late.astype(jnp.bfloat16)
        carry[...] = final
        fan_copy(step).wait()
        acc[...] += lax.dot_general(
            moved(step, tiles, 0),
            both[...],
            (((1,), (1,)), ((), ())),
            preferred_element_type=jnp.float32,
        )
        return unused

    lax.fori_loop(0, count, body, 0)
    tail = jnp.where(part_lane == LANES - 1, carry[...], 0.0).astype(jnp.bfloat16)
    acc[:, channels:] += lax.dot_general(
        moved(count - 1, 1, tiles),
        tail,
        (((1,), (1,)), ((), ())),
        preferred_element_type=jnp.float32,
    )
    outs = []
    for a in range(PAIRS):
        block = acc[a * rows : (a + 1) * rows] * scale
        out_buf[2 * a] = block[:, :channels].astype(out_buf.dtype)
        if a > 0:
            out_buf[2 * a - 1] = block[:, channels:].astype(out_buf.dtype)
        if buffer and a in (PAIRS // 2, PAIRS - 1):
            done = 2 * (PAIRS // 2) + 1 if outs else 0
            span = pl.ds(done, 2 * a + 1 - done)
            outs.append(
                pltpu.make_async_copy(
                    out_buf.at[span], out_hbm.at[out_hbm.shape[0] - 1, span], out_sem.at[len(outs)]
                )
            )
            outs[-1].start()
    for copy in outs:
        copy.wait()


def lagged(place, fan, partner, scale, out_dtype, rounds):
    count, rows = fan.shape[:2]
    channels, length = partner.shape[1:]
    anywhere = pl.BlockSpec(memory_space=pl.ANY)
    buffer = []
    if rounds > 1:
        buffer = [pltpu.VMEM((LAGS, rows, channels), out_dtype), pltpu.SemaphoreType.DMA((2,))]
    return pl.pallas_call(
        functools.partial(lagged_kernel, count, scale),
        out_shape=jax.ShapeDtypeStruct((rounds, LAGS, rows, channels), out_dtype),
        in_specs=[
            pl.BlockSpec(memory_space=pltpu.SMEM),
            anywhere,
            anywhere,
        ],
        out_specs=anywhere if buffer else pl.BlockSpec(memory_space=pltpu.VMEM),
        scratch_shapes=[
            pltpu.VMEM(fan.shape, jnp.bfloat16),
            pltpu.VMEM((2 * channels, length), jnp.bfloat16),
            pltpu.VMEM((channels, LANES), jnp.float32),
            pltpu.VMEM((PAIRS * rows, 2 * channels), jnp.float32),
            pltpu.VMEM((count, channels, length), jnp.bfloat16),
            pltpu.SemaphoreType.DMA((count,)),
            pltpu.SemaphoreType.DMA((count,)),
        ]
        + buffer,
        compiler_params=pltpu.CompilerParams(vmem_limit_bytes=VMEM_BYTES),
        cost_estimate=pl.CostEstimate(
            flops=4 * count * PAIRS * rows * channels * length,
            bytes_accessed=2 * count * channels * length,
            transcendentals=0,
        ),
        name="lagged",
    )(place, fan, partner)


def on_device(raw_strain, band_index, filter_taps):
    channels, length = raw_strain.shape
    count = lax.axis_size("ta")
    rows = channels // count
    scale = 1.0 / math.sqrt(length * count)
    swap = [(0, 1), (1, 0)]
    half, upper, piece = lax.axis_index("zh"), lax.axis_index("cp"), lax.axis_index("ta")

    zero = 0 * piece
    here = jnp.stack([zero, piece % 2, piece, zero + count]).astype(jnp.int32)
    normalized = normalize(raw_strain, band_index, filter_taps, here)
    ring = lax.all_gather(normalized, ("zh", "ta"), axis=0, tiled=False)
    own = lax.all_to_all(normalized.reshape(count, rows, length), "ta", 0, 0)
    guest = lax.ppermute(own, "cp", swap)
    guest_fan, own_fan = fan_of(guest), fan_of(own)

    other = (1 - half) * count
    near = jnp.where(upper == 1, other, half * count)
    place0 = near[None].astype(jnp.int32)
    place1 = other[None].astype(jnp.int32)
    first = lagged(place0, guest_fan, ring, scale, jnp.bfloat16, 1)
    place1, first = lax.optimization_barrier((place1, first))
    first = lax.ppermute(first, "cp", swap)
    result = lagged(place1, own_fan, ring, scale, jnp.float32, ROUNDS)
    return lax.dynamic_update_slice_in_dim(result, first.astype(jnp.float32), 0, 0)


def solution(mesh):
    blocks, slices = mesh.devices.shape
    axes = ("zh", "cp", "col", "ta")
    parts = Mesh(mesh.devices.reshape(2, 2, blocks // 4, slices), axes)
    channel_axes = axes[:3]
    return jax.shard_map(
        on_device,
        mesh=parts,
        in_specs=(P(channel_axes, "ta"), P(channel_axes), P()),
        out_specs=P(None, None, axes, None),
        check_vma=False,
    )
```
